32 devices in a mesh: dp: 8 (over z, x), tensor: 4 (over y, core).
Axes of the slice: x: 2, y: 2, z: 4, core: 2. Of those that a mesh axis runs over, the one named last changes fastest.
Arguments:
- tokens: bfloat16 [8192, 1024], P('dp'), may hold values from -17 to 17
- views: int32 [1], replicated, may hold values from 2 to 8, as said below
- ln1_gain: float32 [1024], replicated, may hold values from 0.5 to 1.5
- ln1_bias: float32 [1024], replicated, may hold values from -3 to 3
- w_query: bfloat16 [1024, 1024], P(None, 'tensor'), may hold values from -0.25 to 0.25
- w_key: bfloat16 [1024, 1024], P(None, 'tensor'), may hold values from -0.25 to 0.25
- w_value: bfloat16 [1024, 1024], P(None, 'tensor'), may hold values from -0.1875 to 0.1875
- w_out: bfloat16 [1024, 1024], P('tensor'), may hold values from -1.5 to 1.5
- ln2_gain: float32 [1024], replicated, may hold values from 0.5 to 1.5
- ln2_bias: float32 [1024], replicated, may hold values from -3 to 3
- w_up: bfloat16 [1024, 4096], P(None, 'tensor'), may hold values from -0.1875 to 0.1875
- w_down: bfloat16 [4096, 1024], P('tensor'), may hold values from -0.09375 to 0.09375
- cotangent: bfloat16 [8192, 1024], P('dp'), may hold values from -6 to 6
Outputs:
- mixed: bfloat16 [8192, 1024], P('dp')
- tokens_grad: bfloat16 [8192, 1024], P('dp')
- ln1_gain_grad: float32 [1024], replicated
- ln1_bias_grad: float32 [1024], replicated
- w_query_grad: float32 [1024, 1024], P(None, 'tensor')
- w_key_grad: float32 [1024, 1024], P(None, 'tensor')
- w_value_grad: float32 [1024, 1024], P(None, 'tensor')
- w_out_grad: float32 [1024, 1024], P('tensor')
- ln2_gain_grad: float32 [1024], replicated
- ln2_bias_grad: float32 [1024], replicated
- w_up_grad: float32 [1024, 4096], P(None, 'tensor')
- w_down_grad: float32 [4096, 1024], P('tensor')
The draws below stay inside these ranges and needn't reach their ends.
Inputs may be any that keep to these rules, and one draw needn't show every extreme that they name: Exactly one scene has 8 views.
All inputs are finite; a program needn't handle non-finite values.
Results may differ from the reference program's by a relative error of at most 0.025.
Values may be sent and summed in bfloat16 or wider, within the bound.
A program may use at most 192 MiB of HBM per device.

```python
import math
import jax
import jax.numpy as jnp
from jax import lax

D = 1024
HEADS = 16
HEAD_DIM = 64
FF = 4096
VIEW_TOK = 1024
MAX_VIEWS = 8
SLOTS = 8192
SCENES = 1
TOKENS = 8192


def draw_tokens(key, part):
    first_key, second_key, third_key = jax.random.split(key, 3)
    base = jnp.clip(jax.random.normal(first_key, (TOKENS, D), jnp.float32), -4.0, 4.0)
    row_scale = jnp.exp(jax.random.uniform(second_key, (TOKENS, 1), jnp.float32, math.log(0.3), math.log(3.0)))
    column_scale = jnp.exp(jax.random.uniform(third_key, (1, D), jnp.float32, math.log(0.7), math.log(1.4)))
    return (base * row_scale * column_scale).astype(jnp.bfloat16)


def draw_views(key, part):
    first_key, second_key = jax.random.split(jax.random.fold_in(key, 17), 2)
    counts = jax.random.randint(first_key, (SCENES,), 2, MAX_VIEWS)
    chosen = jax.random.randint(second_key, (), 0, SCENES)
    return jnp.where(jnp.arange(SCENES) == chosen, MAX_VIEWS, counts).astype(jnp.int32)


def level_of(stream_key, shape, cuts, smallest, top_value):
    def one(axis_at, shards_of):
        steps = jax.random.uniform(jax.random.fold_in(jax.random.fold_in(stream_key, 6), axis_at), (shards_of,), jnp.float32, smallest / len(cuts), top_value / len(cuts))
        return jnp.repeat(jnp.exp(steps), shape[axis_at] // shards_of).reshape((-1,) + (1,) * (len(shape) - axis_at - 1))

    factor_of = one(*cuts[0])
    for cut in cuts[1:]:
        factor_of = factor_of * one(*cut)
    return factor_of


def noise(stream_key, shape, deviation, bound, shards=(), held_as=jnp.bfloat16):
    drawn = jax.random.normal(stream_key, shape, jnp.float32) * deviation
    if len(shards) > 0:
        drawn = level_of(stream_key, shape, shards, -0.22, 0.18) * drawn
    return jnp.clip(drawn, min=-bound, max=bound).astype(held_as)


def setup_inputs(seed: int = 0) -> dict:
    key_list = jax.random.split(jax.random.key(seed), 14)
    return {
        "tokens": draw_tokens(jax.random.fold_in(key_list[13], 71), 0),
        "views": draw_views(jax.random.fold_in(key_list[13], 71), 0),
        "ln1_gain": jnp.clip(1.0 + 0.1 * jax.random.normal(key_list[2], (D,), jnp.float32), 0.5, 1.5),
        "ln1_bias": noise(key_list[3], (D,), 0.5, 3.0, (), jnp.float32),
        "w_query": noise(key_list[4], (D, D), (D // 2) ** -0.5, 0.25, ((1, 4),)),
        "w_key": noise(key_list[5], (D, D), (D // 2) ** -0.5, 0.25, ((1, 4),)),
        "w_value": noise(key_list[6], (D, D), D ** -0.5, 0.1875, ((1, 4),)),
        "w_out": noise(key_list[7], (D, D), (HEAD_DIM // 4) ** -0.5, 1.5, ((0, 4),)),
        "ln2_gain": jnp.clip(1.0 + 0.1 * jax.random.normal(key_list[8], (D,), jnp.float32), 0.5, 1.5),
        "ln2_bias": noise(key_list[9], (D,), 0.5, 3.0, (), jnp.float32),
        "w_up": noise(key_list[10], (D, FF), D ** -0.5, 0.1875, ((1, 4),)),
        "w_down": noise(key_list[11], (FF, D), FF ** -0.5, 0.09375, ((0, 4),)),
        "cotangent": noise(key_list[12], (TOKENS, D), 1.0, 6.0, ((0, 8),)),
    }


highest = lax.Precision.HIGHEST
norm_eps = 1e-05

@jax.custom_vjp
def low(v):
    return lax.optimization_barrier(v.astype(jnp.bfloat16)).astype(jnp.float32)

@jax.custom_vjp
def low_back(v):
    return v

def low_keep(v):
    return (low(v), None)

def low_pass(kept, grad):
    return (grad,)

def back_keep(v):
    return (v, None)

def back_low(kept, grad):
    return (low(grad),)
low.defvjp(low_keep, low_pass)
low_back.defvjp(back_keep, back_low)

def layer_norm(values, gain, shift):
    row_mean = lax.optimization_barrier(jnp.mean(values, axis=-1, keepdims=True))
    centered = values - row_mean
    variance = lax.optimization_barrier(jnp.mean(centered * centered, axis=-1, keepdims=True))
    return centered * lax.rsqrt(variance + norm_eps) * gain + shift

def scene_block(inputs, valid_count, ln1_gain, ln1_bias, w_query, w_key, w_value, w_out, ln2_gain, ln2_bias, w_up, w_down):
    live_keys = jnp.arange(SLOTS, dtype=jnp.int32) < valid_count
    row_keep = live_keys.astype(jnp.float32)[:, None]
    attn_in = low(layer_norm(inputs, ln1_gain, ln1_bias))
    query = low_back(low(jnp.dot(attn_in, w_query, precision=highest)))
    key_rows = low_back(low(jnp.dot(attn_in, w_key, precision=highest)))
    value_rows = low_back(low(jnp.dot(attn_in, w_value, precision=highest)))
    key_heads = key_rows.reshape(SLOTS, HEADS, HEAD_DIM)
    value_heads = value_rows.reshape(SLOTS, HEADS, HEAD_DIM)
    scale_factor = HEAD_DIM ** (-0.5)

    def query_block(query_part):
        scores = low_back(jnp.einsum('qhd,khd->hqk', query_part, key_heads, precision=highest) * scale_factor)
        scores = jnp.where(live_keys[None, None, :], scores, -1000000000.0)
        row_max = lax.optimization_barrier(jnp.max(scores, axis=-1, keepdims=True))
        expon = jnp.exp(scores - row_max)
        probs = expon / lax.optimization_barrier(jnp.sum(expon, axis=-1, keepdims=True))
        return jnp.einsum('hqk,khd->qhd', low(probs), value_heads, precision=highest)
    block_rows = math.gcd(SLOTS, 512)
    query_heads = query.reshape(SLOTS // block_rows, block_rows, HEADS, HEAD_DIM)
    heads_out = lax.map(jax.checkpoint(query_block), query_heads)
    attn_heads = low_back(low(heads_out.reshape(SLOTS, D)))
    attn_proj = low_back(jnp.dot(attn_heads, w_out, precision=highest))
    resid = inputs + row_keep * attn_proj
    mlp_in = low(layer_norm(resid, ln2_gain, ln2_bias))
    up_proj = low_back(jnp.dot(mlp_in, w_up, precision=highest))
    act_low = low(jax.nn.gelu(up_proj, approximate=True))
    mlp_proj = low_back(jnp.dot(act_low, w_down, precision=highest))
    return resid + row_keep * mlp_proj

def reference(tokens, views, ln1_gain, ln1_bias, w_query, w_key, w_value, w_out, ln2_gain, ln2_bias, w_up, w_down, cotangent):
    weights_all = tuple((weight.astype(jnp.float32) for weight in (ln1_gain, ln1_bias, w_query, w_key, w_value, w_out, ln2_gain, ln2_bias, w_up, w_down)))
    inputs = tokens.astype(jnp.float32).reshape(SCENES, SLOTS, D)
    valid_counts = (views * VIEW_TOK).astype(jnp.int32)

    def forward(scene_inputs, *weight_list):

        def one_scene(scene_item):
            return scene_block(scene_item[0], scene_item[1], *weight_list)
        return lax.map(one_scene, (scene_inputs, valid_counts))
    outcome, pullback = jax.vjp(forward, inputs, *weights_all)
    gradients = pullback(cotangent.astype(jnp.float32).reshape(SCENES, SLOTS, D))
    mixed = outcome.reshape(TOKENS, D).astype(jnp.bfloat16)
    tokens_grad = gradients[0].reshape(TOKENS, D).astype(jnp.bfloat16)
    return (mixed, tokens_grad, gradients[1], gradients[2], gradients[3], gradients[4], gradients[5], gradients[6], gradients[7], gradients[8], gradients[9], gradients[10])
```

```python
from functools import partial
import math

import jax
import jax.numpy as jnp
from jax import lax
from jax.experimental import pallas as pl
from jax.experimental.pallas import tpu as pltpu
from jax.sharding import PartitionSpec as P

HEAD_DIM = 64
VIEW_TOK = 1024
MAX_VIEWS = 8
LOG2E = math.log2(math.e)
VMEM_BYTES = 56 << 20

norm_eps = 1e-05
bf16 = jnp.bfloat16
f32 = jnp.float32
dot = partial(jnp.dot, preferred_element_type=f32)


def contract(left, right, left_dim, right_dim):
    return lax.dot_general(
        left, right, (((left_dim,), (right_dim,)), ((), ())), preferred_element_type=f32
    )


def layer_norm(values, gain, shift):
    row_mean = jnp.mean(values, axis=-1, keepdims=True)
    centered = values - row_mean
    inverse = lax.rsqrt(jnp.mean(centered * centered, axis=-1, keepdims=True) + norm_eps)
    normed = centered * inverse
    return (normed * gain + shift, normed, inverse)


def norm_back(grad_norm, normed, inverse, gain):
    scaled = grad_norm * gain
    grad_input = inverse * (
        scaled
        - jnp.mean(scaled, axis=-1, keepdims=True)
        - normed * jnp.mean(scaled * normed, axis=-1, keepdims=True)
    )
    return (grad_input, jnp.sum(grad_norm * normed, axis=0), jnp.sum(grad_norm, axis=0))


def sweep_forward(live_views, q_pad, kv, v_ones, carry, last):
    count = q_pad.shape[1]
    keys = kv.shape[0]
    sum_rows = v_ones.shape[0]
    bq, bk = 2048, 512

    def kernel(*refs):
        live_ref, q_ref, kv_ref, v_ref = refs[:4]
        refs = refs[4:]
        if carry is not None:
            start = (refs[0][...], refs[1][...])
            refs = refs[2:]
        else:
            start = (jnp.full((1, bq), -1e30, f32), jnp.zeros((sum_rows, bq), f32))
        queries = q_ref[...]

        def view_step(view, running):
            top, accum = running
            for part in range(VIEW_TOK // bk):
                first = pl.multiple_of(view * VIEW_TOK + part * bk, bk)
                scores = dot(kv_ref[pl.ds(first, bk), :], queries)
                new_top = jnp.maximum(top, jnp.max(scores, axis=0, keepdims=True))
                weights = jnp.exp2(scores - new_top).astype(bf16)
                accum = accum * jnp.exp2(top - new_top) + dot(v_ref[:, pl.ds(first, bk)], weights)
                top = new_top
            return (top, accum)

        top, accum = lax.fori_loop(0, live_ref[0], view_step, start)
        if last:
            total = accum[HEAD_DIM : HEAD_DIM + 1]
            heads_out = accum[:HEAD_DIM] / total
            refs[0][...] = heads_out
            refs[1][...] = heads_out.astype(bf16)
            refs[2][...] = top + jnp.log2(total)
        else:
            refs[0][...] = top
            refs[1][...] = accum

    def columns(rows):
        return pl.BlockSpec((rows, bq), lambda i: (0, i))

    whole = [
        pl.BlockSpec((keys, kv.shape[1]), lambda i: (0, 0)),
        pl.BlockSpec((sum_rows, keys), lambda i: (0, 0)),
    ]
    in_specs = [pl.BlockSpec(memory_space=pltpu.SMEM), columns(q_pad.shape[0])] + whole
    operands = [live_views, q_pad, kv, v_ones]
    if carry is not None:
        in_specs += [columns(1), columns(sum_rows)]
        operands += list(carry)
    if last:
        shapes = [((HEAD_DIM, count), f32), ((HEAD_DIM, count), bf16), ((1, count), f32)]
    else:
        shapes = [((1, count), f32), ((sum_rows, count), f32)]
    return pl.pallas_call(
        kernel,
        grid=(count // bq,),
        in_specs=in_specs,
        out_specs=[columns(shape[0]) for shape, _ in shapes],
        out_shape=[jax.ShapeDtypeStruct(shape, kind) for shape, kind in shapes],
        compiler_params=pltpu.CompilerParams(vmem_limit_bytes=VMEM_BYTES),
        cost_estimate=pl.CostEstimate(
            flops=16 * HEAD_DIM * count * keys, bytes_accessed=8 << 20, transcendentals=count * keys
        ),
    )(*operands)


def sweep_backward(live_views, q_pad, g_pad, q_rows, g_rows, kv, k_cols, log_norm, delta, carry):
    count = q_pad.shape[1]
    keys = kv.shape[0]
    bq, bk = 1024, 512
    last = carry is not None

    def kernel(*refs):
        live_ref, q_ref, g_ref, qr_ref, gr_ref, kv_ref, kc_ref, norm_ref, delta_ref = refs[:9]
        carry_ref = refs[9] if last else None
        pairs_ref, out_ref, total_ref = refs[-3:]
        step = pl.program_id(0)

        @pl.when(step == 0)
        def _():
            total_ref[...] = carry_ref[...] if last else jnp.zeros_like(total_ref)

        live = step * bk < live_ref[0] * VIEW_TOK

        @pl.when(live)
        def _():
            key_values = kv_ref[...]
            key_columns = kc_ref[...]
            accum = jnp.zeros((bk, 2 * HEAD_DIM), f32)
            for part in range(count // bq):
                span = pl.ds(part * bq, bq)
                scores = dot(key_values, q_ref[:, span])
                weights = jnp.exp2(scores - norm_ref[:, span])
                grad_weights = dot(key_values, g_ref[:, span])
                grad_scores = (weights * (grad_weights - delta_ref[:, span])).astype(bf16)
                accum += dot(weights.astype(bf16), gr_ref[span, :])
                accum += dot(grad_scores, qr_ref[span, :])
                total_ref[:, span] += dot(key_columns, grad_scores)
            lane = lax.broadcasted_iota(jnp.int32, accum.shape, 1)
            pairs_ref[...] = jnp.where(lane < HEAD_DIM, accum * (1.0 / LOG2E), accum).astype(bf16)

        @pl.when(jnp.logical_not(live))
        def _():
            pairs_ref[...] = jnp.zeros_like(pairs_ref)

        @pl.when(step == pl.num_programs(0) - 1)
        def _():
            if last:
                out_ref[...] = (total_ref[...] * HEAD_DIM ** (-0.5)).astype(bf16)
            else:
                out_ref[...] = total_ref[...]

    def whole(array):
        return pl.BlockSpec(array.shape, lambda i: (0, 0))

    in_specs = [
        pl.BlockSpec(memory_space=pltpu.SMEM),
        whole(q_pad),
        whole(g_pad),
        whole(q_rows),
        whole(g_rows),
        pl.BlockSpec((bk, 2 * HEAD_DIM), lambda i: (i, 0)),
        pl.BlockSpec((HEAD_DIM, bk), lambda i: (0, i)),
        whole(log_norm),
        whole(delta),
    ]
    operands = [live_views, q_pad, g_pad, q_rows, g_rows, kv, k_cols, log_norm, delta]
    if last:
        in_specs.append(whole(carry))
        operands.append(carry)
    return pl.pallas_call(
        kernel,
        grid=(keys // bk,),
        in_specs=in_specs,
        out_specs=[
            pl.BlockSpec((bk, 2 * HEAD_DIM), lambda i: (i, 0)),
            pl.BlockSpec((HEAD_DIM, count), lambda i: (0, 0)),
        ],
        out_shape=[
            jax.ShapeDtypeStruct((keys, 2 * HEAD_DIM), bf16),
            jax.ShapeDtypeStruct((HEAD_DIM, count), bf16 if last else f32),
        ],
        scratch_shapes=[pltpu.VMEM((HEAD_DIM, count), f32)],
        compiler_params=pltpu.CompilerParams(vmem_limit_bytes=VMEM_BYTES),
        cost_estimate=pl.CostEstimate(
            flops=40 * HEAD_DIM * count * keys, bytes_accessed=10 << 20, transcendentals=count * keys
        ),
    )(*operands)


def shards(
    tokens,
    views,
    ln1_gain,
    ln1_bias,
    w_query,
    w_key,
    w_value,
    w_out,
    ln2_gain,
    ln2_bias,
    w_up,
    w_down,
    cotangent,
):
    row_count, width = tokens.shape
    inner = w_query.shape[1]
    heads = inner // HEAD_DIM
    half = row_count // 2
    group = MAX_VIEWS * VIEW_TOK // row_count
    devices = lax.axis_size("dp")
    assert row_count == VIEW_TOK and group == 2 * heads and lax.axis_size("tensor") == 4
    position = lax.axis_index("dp")
    block = position % group
    side = block % 2
    core = lax.axis_index("tensor") % 2
    scene_views = lax.dynamic_index_in_dim(views, position // group, keepdims=False)
    own_views = ((scene_views + 1 - side) // 2).reshape(1)
    far_views = ((scene_views + side) // 2).reshape(1)
    keep = (block < scene_views).astype(f32)
    lanes = [
        [first + 2 * place + bit for place in range(heads)]
        for first in range(0, devices, group)
        for bit in range(2)
    ]

    def exchange(block, split, concat):
        return lax.all_to_all(
            block, "dp", split, concat, axis_index_groups=lanes, tiled=True
        )

    def across(block):
        return lax.ppermute(block, "dp", [(i, i ^ 1) for i in range(devices)])

    def other_core(block):
        return lax.ppermute(block, "tensor", [(i, i ^ 1) for i in range(4)])

    def other_chip(block):
        return lax.ppermute(block, "tensor", [(i, i ^ 2) for i in range(4)])

    def own_first(block):
        return jnp.where(core == 0, block, jnp.concatenate([block[half:], block[:half]], axis=0))

    def own_rows_sum(far_part, own_part):
        arrived = other_core(far_part().astype(bf16))
        pair = (own_part() + arrived.astype(f32)).astype(bf16)
        return pair.astype(f32) + other_chip(pair).astype(f32)

    def both_halves(own):
        return jnp.concatenate([own, other_core(own)], axis=0)

    rows = own_first(tokens)
    grad_rows = own_first(cotangent)
    inputs_own = rows[:half].astype(f32)
    grad_own = grad_rows[:half].astype(f32)

    attn_norm, normed_first, inverse_first = layer_norm(rows.astype(f32), ln1_gain, ln1_bias)
    attn_in = attn_norm.astype(bf16)
    w_pairs = jnp.concatenate(
        [w_key.reshape(width, heads, HEAD_DIM), w_value.reshape(width, heads, HEAD_DIM)], axis=2
    ).reshape(width, 2 * inner)
    kv_low = dot(attn_in, w_pairs).astype(bf16)
    kv_own = exchange(kv_low, 1, 0)
    query_low = (contract(w_query, attn_in, 0, 1) * (LOG2E * HEAD_DIM ** (-0.5))).astype(bf16)
    q_cols = exchange(query_low, 0, 1)
    kv_far = across(kv_own)

    empty = jnp.zeros_like(q_cols)
    q_pad = jnp.concatenate([q_cols, empty], axis=0)

    def value_columns(kv):
        cols = kv.T
        ones = jnp.ones((16, cols.shape[1]), bf16)
        return cols[:HEAD_DIM], jnp.concatenate([cols[HEAD_DIM:], ones], axis=0)

    k_own, v_own = value_columns(kv_own)
    carry = sweep_forward(own_views, q_pad, kv_own, v_own, None, False)
    k_far, v_far = value_columns(kv_far)
    heads_out, heads_low, log_norm = sweep_forward(far_views, q_pad, kv_far, v_far, carry, True)
    attn_cols = exchange(heads_low, 1, 0)

    resid = inputs_own + keep * own_rows_sum(
        lambda: contract(attn_cols[:, half:], w_out, 0, 0),
        lambda: contract(attn_cols[:, :half], w_out, 0, 0),
    )
    mlp_norm, normed_second, inverse_second = layer_norm(resid, ln2_gain, ln2_bias)
    mlp_in = both_halves(mlp_norm.astype(bf16))
    up_proj = dot(mlp_in, w_up)
    activated, gelu_pull = jax.vjp(partial(jax.nn.gelu, approximate=True), up_proj)
    act_low = activated.astype(bf16)
    grad_mlp = (keep * grad_rows.astype(f32)).astype(bf16)
    grad_act = contract(grad_mlp, w_down, 1, 1)
    grad_up = gelu_pull(grad_act)[0].astype(bf16)
    grad_mlp_in = own_rows_sum(
        lambda: contract(grad_up[half:], w_up, 1, 1), lambda: contract(grad_up[:half], w_up, 1, 1)
    )
    mlp_proj = own_rows_sum(
        lambda: dot(act_low[half:], w_down), lambda: dot(act_low[:half], w_down)
    )
    mixed_own = (resid + keep * mlp_proj).astype(bf16)
    grad_second, ln2_gain_grad, ln2_bias_grad = norm_back(
        grad_mlp_in, normed_second, inverse_second, ln2_gain
    )
    grad_resid = grad_own + grad_second
    grad_attn = both_halves((keep * grad_resid).astype(bf16))
    grad_heads = contract(w_out, grad_attn, 1, 1).astype(bf16)
    g_cols = exchange(grad_heads, 0, 1)

    w_down_grad = contract(act_low, grad_mlp, 0, 0)
    w_up_grad = contract(mlp_in, grad_up, 0, 0)
    w_out_grad = dot(attn_cols, grad_attn)
    early = lax.psum((w_up_grad.astype(bf16), w_down_grad.astype(bf16), w_out_grad.astype(bf16)), "dp")

    g_pad = jnp.concatenate([empty, g_cols], axis=0)
    delta = jnp.sum(g_cols.astype(f32) * heads_out, axis=0, keepdims=True)
    q_rows = q_pad.T
    g_rows = g_pad.T
    pairs_far, carry = sweep_backward(
        far_views, q_pad, g_pad, q_rows, g_rows, kv_far, k_far, log_norm, delta, None
    )
    arrived = across(pairs_far)
    pairs_own, dq_cols = sweep_backward(
        own_views, q_pad, g_pad, q_rows, g_rows, kv_own, k_own, log_norm, delta, carry
    )
    pairs = (pairs_own.astype(f32) + arrived.astype(f32)).astype(bf16)
    grad_pairs = exchange(
        pairs.reshape(heads, row_count, 2 * HEAD_DIM), 0, 2
    ).reshape(row_count, 2 * inner)
    grad_query = exchange(dq_cols, 1, 0)

    def partial_in(start):
        return contract(grad_query[:, start : start + half], w_query, 0, 1) + contract(
            grad_pairs[start : start + half], w_pairs, 1, 1
        )

    grad_attn_in = own_rows_sum(lambda: partial_in(half), lambda: partial_in(0))
    grad_first, ln1_gain_grad, ln1_bias_grad = norm_back(
        grad_attn_in, normed_first[:half], inverse_first[:half], ln1_gain
    )
    tokens_grad_own = (grad_resid + grad_first).astype(bf16)

    w_query_grad = contract(attn_in, grad_query, 0, 1)
    w_pairs_grad = contract(attn_in, grad_pairs, 0, 0)
    late, early = lax.optimization_barrier(
        ((w_query_grad.astype(bf16), w_pairs_grad.astype(bf16)), early)
    )
    late = lax.psum(late, "dp")
    w_pairs_grad = late[1].astype(f32).reshape(width, heads, 2 * HEAD_DIM)
    small = jnp.stack([ln1_gain_grad, ln1_bias_grad, ln2_gain_grad, ln2_bias_grad]) * 0.5
    small = lax.psum(small, ("dp", "tensor"))

    def in_order(own):
        far = other_core(own)
        return jnp.where(
            core == 0, jnp.concatenate([own, far], axis=0), jnp.concatenate([far, own], axis=0)
        )

    return (
        in_order(mixed_own),
        in_order(tokens_grad_own),
        small[0],
        small[1],
        late[0].astype(f32),
        w_pairs_grad[:, :, :HEAD_DIM].reshape(width, inner),
        w_pairs_grad[:, :, HEAD_DIM:].reshape(width, inner),
        early[2].astype(f32),
        small[2],
        small[3],
        early[0].astype(f32),
        early[1].astype(f32),
    )


def solution(mesh):
    placed = (
        P("dp", None),
        P(),
        P(),
        P(),
        P(None, "tensor"),
        P(None, "tensor"),
        P(None, "tensor"),
        P("tensor", None),
        P(),
        P(),
        P(None, "tensor"),
        P("tensor", None),
        P("dp", None),
    )
    return jax.shard_map(
        shards,
        mesh=mesh,
        in_specs=placed,
        out_specs=(
            P("dp", None),
            P("dp", None),
            P(),
            P(),
            P(None, "tensor"),
            P(None, "tensor"),
            P(None, "tensor"),
            P("tensor", None),
            P(),
            P(),
            P(None, "tensor"),
            P("tensor", None),
        ),
        check_vma=False,
    )
```

```python
from functools import partial
import math

import jax
import jax.numpy as jnp
from jax import lax
from jax.experimental import pallas as pl
from jax.experimental.pallas import tpu as pltpu
from jax.sharding import PartitionSpec as P

HEAD_DIM = 64
VIEW_TOK = 1024
MAX_VIEWS = 8
LOG2E = math.log2(math.e)
VMEM_BYTES = 56 << 20

norm_eps = 1e-05

bf16 = jnp.bfloat16
f32 = jnp.float32
dot = partial(jnp.dot, preferred_element_type=f32)


def contract(left, right, left_dim, right_dim):
    return lax.dot_general(
        left, right, (((left_dim,), (right_dim,)), ((), ())), preferred_element_type=f32
    )


def layer_norm(values, gain, shift):
    row_mean = jnp.mean(values, axis=-1, keepdims=True)
    centered = values - row_mean
    inverse = lax.rsqrt(jnp.mean(centered * centered, axis=-1, keepdims=True) + norm_eps)
    normed = centered * inverse
    return (normed * gain + shift, normed, inverse)


def norm_back(grad_norm, normed, inverse, gain):
    scaled = grad_norm * gain
    grad_input = inverse * (
        scaled
        - jnp.mean(scaled, axis=-1, keepdims=True)
        - normed * jnp.mean(scaled * normed, axis=-1, keepdims=True)
    )
    return (grad_input, jnp.sum(grad_norm * normed, axis=0), jnp.sum(grad_norm, axis=0))


def sweep_forward(live_views, q_pad, kv, v_ones, carry, last):
    count = q_pad.shape[1]
    keys = kv.shape[0]
    sum_rows = v_ones.shape[0]
    bq, bk = 2048, 512

    def kernel(*refs):
        live_ref, q_ref, kv_ref, v_ref = refs[:4]
        refs = refs[4:]
        if carry is not None:
            start = (refs[0][...], refs[1][...])
            refs = refs[2:]
        else:
            start = (jnp.full((1, bq), -1e30, f32), jnp.zeros((sum_rows, bq), f32))
        queries = q_ref[...]

        def view_step(view, running):
            top, accum = running
            for part in range(VIEW_TOK // bk):
                first = pl.multiple_of(view * VIEW_TOK + part * bk, bk)
                scores = dot(kv_ref[pl.ds(first, bk), :], queries)
                new_top = jnp.maximum(top, jnp.max(scores, axis=0, keepdims=True))
                weights = jnp.exp2(scores - new_top).astype(bf16)
                accum = accum * jnp.exp2(top - new_top) + dot(v_ref[:, pl.ds(first, bk)], weights)
                top = new_top
            return (top, accum)

        top, accum = lax.fori_loop(0, live_ref[0], view_step, start)
        if last:
            total = accum[HEAD_DIM : HEAD_DIM + 1]
            heads_out = accum[:HEAD_DIM] / total
            refs[0][...] = heads_out
            refs[1][...] = heads_out.astype(bf16)
            refs[2][...] = top + jnp.log2(total)
        else:
            refs[0][...] = top
            refs[1][...] = accum

    def columns(rows):
        return pl.BlockSpec((rows, bq), lambda i: (0, i))

    whole = [
        pl.BlockSpec((keys, kv.shape[1]), lambda i: (0, 0)),
        pl.BlockSpec((sum_rows, keys), lambda i: (0, 0)),
    ]
    in_specs = [pl.BlockSpec(memory_space=pltpu.SMEM), columns(q_pad.shape[0])] + whole
    operands = [live_views, q_pad, kv, v_ones]
    if carry is not None:
        in_specs += [columns(1), columns(sum_rows)]
        operands += list(carry)
    if last:
        shapes = [((HEAD_DIM, count), f32), ((HEAD_DIM, count), bf16), ((1, count), f32)]
    else:
        shapes = [((1, count), f32), ((sum_rows, count), f32)]
    return pl.pallas_call(
        kernel,
        grid=(count // bq,),
        in_specs=in_specs,
        out_specs=[columns(shape[0]) for shape, _ in shapes],
        out_shape=[jax.ShapeDtypeStruct(shape, kind) for shape, kind in shapes],
        compiler_params=pltpu.CompilerParams(vmem_limit_bytes=VMEM_BYTES),
        cost_estimate=pl.CostEstimate(
            flops=16 * HEAD_DIM * count * keys, bytes_accessed=8 << 20, transcendentals=count * keys
        ),
    )(*operands)


def sweep_backward(live_views, q_pad, g_pad, q_rows, g_rows, kv, k_cols, log_norm, delta, carry):
    count = q_pad.shape[1]
    keys = kv.shape[0]
    bq, bk = 1024, 512
    last = carry is not None

    def kernel(*refs):
        live_ref, q_ref, g_ref, qr_ref, gr_ref, kv_ref, kc_ref, norm_ref, delta_ref = refs[:9]
        carry_ref = refs[9] if last else None
        pairs_ref, out_ref, total_ref = refs[-3:]
        step = pl.program_id(0)

        @pl.when(step == 0)
        def _():
            total_ref[...] = carry_ref[...] if last else jnp.zeros_like(total_ref)

        live = step * bk < live_ref[0] * VIEW_TOK

        @pl.when(live)
        def _():
            key_values = kv_ref[...]
            key_columns = kc_ref[...]
            accum = jnp.zeros((bk, 2 * HEAD_DIM), f32)
            for part in range(count // bq):
                span = pl.ds(part * bq, bq)
                scores = dot(key_values, q_ref[:, span])
                weights = jnp.exp2(scores - norm_ref[:, span])
                grad_weights = dot(key_values, g_ref[:, span])
                grad_scores = (weights * (grad_weights - delta_ref[:, span])).astype(bf16)
                accum += dot(weights.astype(bf16), gr_ref[span, :])
                accum += dot(grad_scores, qr_ref[span, :])
                total_ref[:, span] += dot(key_columns, grad_scores)
            lane = lax.broadcasted_iota(jnp.int32, accum.shape, 1)
            pairs_ref[...] = jnp.where(lane < HEAD_DIM, accum * (1.0 / LOG2E), accum).astype(bf16)

        @pl.when(jnp.logical_not(live))
        def _():
            pairs_ref[...] = jnp.zeros_like(pairs_ref)

        @pl.when(step == pl.num_programs(0) - 1)
        def _():
            if last:
                out_ref[...] = (total_ref[...] * HEAD_DIM ** (-0.5)).astype(bf16)
            else:
                out_ref[...] = total_ref[...]

    def whole(array):
        return pl.BlockSpec(array.shape, lambda i: (0, 0))

    in_specs = [
        pl.BlockSpec(memory_space=pltpu.SMEM),
        whole(q_pad),
        whole(g_pad),
        whole(q_rows),
        whole(g_rows),
        pl.BlockSpec((bk, 2 * HEAD_DIM), lambda i: (i, 0)),
        pl.BlockSpec((HEAD_DIM, bk), lambda i: (0, i)),
        whole(log_norm),
        whole(delta),
    ]
    operands = [live_views, q_pad, g_pad, q_rows, g_rows, kv, k_cols, log_norm, delta]
    if last:
        in_specs.append(whole(carry))
        operands.append(carry)
    return pl.pallas_call(
        kernel,
        grid=(keys // bk,),
        in_specs=in_specs,
        out_specs=[
            pl.BlockSpec((bk, 2 * HEAD_DIM), lambda i: (i, 0)),
            pl.BlockSpec((HEAD_DIM, count), lambda i: (0, 0)),
        ],
        out_shape=[
            jax.ShapeDtypeStruct((keys, 2 * HEAD_DIM), bf16),
            jax.ShapeDtypeStruct((HEAD_DIM, count), bf16 if last else f32),
        ],
        scratch_shapes=[pltpu.VMEM((HEAD_DIM, count), f32)],
        compiler_params=pltpu.CompilerParams(vmem_limit_bytes=VMEM_BYTES),
        cost_estimate=pl.CostEstimate(
            flops=40 * HEAD_DIM * count * keys, bytes_accessed=10 << 20, transcendentals=count * keys
        ),
    )(*operands)


def shards(
    tokens,
    views,
    ln1_gain,
    ln1_bias,
    w_query,
    w_key,
    w_value,
    w_out,
    ln2_gain,
    ln2_bias,
    w_up,
    w_down,
    cotangent,
):
    row_count, width = tokens.shape
    inner = w_query.shape[1]
    heads = inner // HEAD_DIM
    half = row_count // 2
    group = MAX_VIEWS * VIEW_TOK // row_count
    devices = lax.axis_size("dp")
    assert row_count == VIEW_TOK and group == 2 * heads and lax.axis_size("tensor") == 4
    position = lax.axis_index("dp")
    block = position % group
    side = block % 2
    core = lax.axis_index("tensor") % 2
    scene_views = lax.dynamic_index_in_dim(views, position // group, keepdims=False)
    own_views = ((scene_views + 1 - side) // 2).reshape(1)
    far_views = ((scene_views + side) // 2).reshape(1)
    keep = (block < scene_views).astype(f32)
    lanes = [
        [first + 2 * place + bit for place in range(heads)]
        for first in range(0, devices, group)
        for bit in range(2)
    ]

    def exchange(block, split, concat):
        return lax.all_to_all(
            block, "dp", split, concat, axis_index_groups=lanes, tiled=True
        )

    def across(block):
        return lax.ppermute(block, "dp", [(i, i ^ 1) for i in range(devices)])

    def other_core(block):
        return lax.ppermute(block, "tensor", [(i, i ^ 1) for i in range(4)])

    def other_chip(block):
        return lax.ppermute(block, "tensor", [(i, i ^ 2) for i in range(4)])

    def own_first(block):
        return jnp.where(core == 0, block, jnp.concatenate([block[half:], block[:half]], axis=0))

    def pair_sum(far_part, own_part):
        arrived = other_core(far_part.astype(bf16))
        return (own_part + arrived.astype(f32)).astype(bf16)

    def with_small(grad, *parts):
        parts = [part.astype(bf16)[None] for part in parts]
        return jnp.concatenate([grad] + parts + [jnp.zeros((14, width), bf16)], axis=0)

    def both_halves(own):
        return jnp.concatenate([own, other_core(own)], axis=0)

    rows = own_first(tokens)
    grad_rows = own_first(cotangent)
    inputs_own = rows[:half].astype(f32)
    grad_own = grad_rows[:half].astype(f32)

    attn_norm, normed_first, inverse_first = layer_norm(rows.astype(f32), ln1_gain, ln1_bias)
    attn_in = attn_norm.astype(bf16)
    w_pairs = jnp.concatenate(
        [w_key.reshape(width, heads, HEAD_DIM), w_value.reshape(width, heads, HEAD_DIM)], axis=2
    ).reshape(width, 2 * inner)
    kv_low = dot(attn_in, w_pairs).astype(bf16)
    kv_own = exchange(kv_low, 1, 0)
    query_low = (contract(w_query, attn_in, 0, 1) * (LOG2E * HEAD_DIM ** (-0.5))).astype(bf16)
    q_cols = exchange(query_low, 0, 1)
    kv_far = across(kv_own)

    empty = jnp.zeros_like(q_cols)
    q_pad = jnp.concatenate([q_cols, empty], axis=0)

    def value_columns(kv):
        cols = kv.T
        ones = jnp.ones((16, cols.shape[1]), bf16)
        return cols[:HEAD_DIM], jnp.concatenate([cols[HEAD_DIM:], ones], axis=0)

    k_own, v_own = value_columns(kv_own)
    carry = sweep_forward(own_views, q_pad, kv_own, v_own, None, False)
    k_far, v_far = value_columns(kv_far)
    heads_out, heads_low, log_norm = sweep_forward(far_views, q_pad, kv_far, v_far, carry, True)
    attn_cols = exchange(heads_low, 1, 0)

    pair = pair_sum(
        contract(attn_cols[:, half:], w_out, 0, 0), contract(attn_cols[:, :half], w_out, 0, 0)
    )
    resid = inputs_own + keep * (pair.astype(f32) + other_chip(pair).astype(f32))
    mlp_norm, normed_second, inverse_second = layer_norm(resid, ln2_gain, ln2_bias)
    mlp_in = both_halves(mlp_norm.astype(bf16))
    grad_mlp = (keep * grad_rows.astype(f32)).astype(bf16)
    grad_act = lax.optimization_barrier(contract(grad_mlp, w_down, 1, 1))
    up_proj = dot(mlp_in, w_up)
    activated, gelu_pull = jax.vjp(partial(jax.nn.gelu, approximate=True), up_proj)
    act_low = activated.astype(bf16)
    grad_up = gelu_pull(grad_act)[0].astype(bf16)
    pair = pair_sum(contract(grad_up[half:], w_up, 1, 1), contract(grad_up[:half], w_up, 1, 1))
    w_down_grad = contract(act_low, grad_mlp, 0, 0).astype(bf16)
    w_up_grad = contract(mlp_in, grad_up, 0, 0).astype(bf16)
    arrived, act_low, w_up_grad, w_down_grad = lax.optimization_barrier(
        (other_chip(pair), act_low, w_up_grad, w_down_grad)
    )
    early = lax.psum((w_up_grad, w_down_grad), "dp")
    grad_mlp_in = pair.astype(f32) + arrived.astype(f32)
    mlp_pair = pair_sum(dot(act_low[half:], w_down), dot(act_low[:half], w_down))
    mlp_arrived = other_chip(mlp_pair)
    grad_second, ln2_gain_grad, ln2_bias_grad = norm_back(
        grad_mlp_in, normed_second, inverse_second, ln2_gain
    )
    grad_resid = grad_own + grad_second
    grad_attn = both_halves((keep * grad_resid).astype(bf16))
    grad_heads = contract(w_out, grad_attn, 1, 1).astype(bf16)
    g_cols = exchange(grad_heads, 0, 1)
    w_out_grad = dot(attn_cols, grad_attn).astype(bf16)
    middle = lax.psum(
        with_small(w_out_grad, ln2_gain_grad * 0.5, ln2_bias_grad * 0.5),
        "dp",
        axis_index_groups=[list(range(devices))[::-1]],
    )

    g_pad = jnp.concatenate([empty, g_cols], axis=0)
    delta = jnp.sum(g_cols.astype(f32) * heads_out, axis=0, keepdims=True)
    q_rows = q_pad.T
    g_rows = g_pad.T
    pairs_far, carry = sweep_backward(
        far_views, q_pad, g_pad, q_rows, g_rows, kv_far, k_far, log_norm, delta, None
    )
    resid, mlp_pair, mlp_arrived, pairs_far = lax.optimization_barrier(
        (resid, mlp_pair, mlp_arrived, pairs_far)
    )
    mixed_own = (
        resid + keep * (mlp_pair.astype(f32) + mlp_arrived.astype(f32))
    ).astype(bf16)
    arrived = across(pairs_far)
    pairs_own, dq_cols = sweep_backward(
        own_views, q_pad, g_pad, q_rows, g_rows, kv_own, k_own, log_norm, delta, carry
    )
    pairs = (pairs_own.astype(f32) + arrived.astype(f32)).astype(bf16)
    grad_query = exchange(dq_cols, 1, 0)
    grad_pairs = exchange(
        pairs.reshape(heads, row_count, 2 * HEAD_DIM), 0, 2
    ).reshape(row_count, 2 * inner)

    grad_pairs, early, middle = lax.optimization_barrier((grad_pairs, early, middle))

    def partial_in(start):
        return contract(grad_query[:, start : start + half], w_query, 0, 1) + contract(
            grad_pairs[start : start + half], w_pairs, 1, 1
        )

    far_part, own_part = partial_in(half), partial_in(0)
    late = (
        contract(attn_in, grad_pairs, 0, 0).astype(bf16),
        with_small(
            dot(grad_query, attn_in).astype(bf16),
            jnp.sum(far_part * normed_first[half:], axis=0)
            + jnp.sum(own_part * normed_first[:half], axis=0),
            jnp.sum(far_part, axis=0) + jnp.sum(own_part, axis=0),
        ),
    )
    arrived, late = lax.optimization_barrier((other_core(far_part.astype(bf16)), late))
    late = lax.psum(late, "dp")
    pair = (own_part + arrived.astype(f32)).astype(bf16)
    grad_attn_in = pair.astype(f32) + other_chip(pair).astype(f32)
    grad_first, _, _ = norm_back(
        grad_attn_in, normed_first[:half], inverse_first[:half], ln1_gain
    )
    tokens_grad_own = (grad_resid + grad_first).astype(bf16)
    w_pairs_grad = late[0].astype(f32).reshape(width, heads, 2 * HEAD_DIM)
    small = jnp.concatenate([late[1][inner:], middle[inner:]], axis=0).astype(f32)
    small = small + other_core(small)
    small = small + other_chip(small)

    def in_order(own):
        far = other_core(own)
        return jnp.where(
            core == 0, jnp.concatenate([own, far], axis=0), jnp.concatenate([far, own], axis=0)
        )

    return (
        in_order(mixed_own),
        in_order(tokens_grad_own),
        small[0],
        small[1],
        late[1][:inner].astype(f32).T,
        w_pairs_grad[:, :, :HEAD_DIM].reshape(width, inner),
        w_pairs_grad[:, :, HEAD_DIM:].reshape(width, inner),
        middle[:inner].astype(f32),
        small[16],
        small[17],
        early[0].astype(f32),
        early[1].astype(f32),
    )


def solution(mesh):
    placed = (
        P("dp", None),
        P(),
        P(),
        P(),
        P(None, "tensor"),
        P(None, "tensor"),
        P(None, "tensor"),
        P("tensor", None),
        P(),
        P(),
        P(None, "tensor"),
        P("tensor", None),
        P("dp", None),
    )
    return jax.shard_map(
        shards,
        mesh=mesh,
        in_specs=placed,
        out_specs=(
            P("dp", None),
            P("dp", None),
            P(),
            P(),
            P(None, "tensor"),
            P(None, "tensor"),
            P(None, "tensor"),
            P("tensor", None),
            P(),
            P(),
            P(None, "tensor"),
            P("tensor", None),
        ),
        check_vma=False,
    )
```

```python
from functools import partial
import math

import jax
import jax.numpy as jnp
from jax import lax
from jax.experimental import pallas as pl
from jax.experimental.pallas import tpu as pltpu
from jax.sharding import PartitionSpec as P

HEAD_DIM = 64
VIEW_TOK = 1024
MAX_VIEWS = 8
LOG2E = math.log2(math.e)
VMEM_BYTES = 56 << 20

norm_eps = 1e-05

bf16 = jnp.bfloat16
f32 = jnp.float32
dot = partial(jnp.dot, preferred_element_type=f32)


def contract(left, right, left_dim, right_dim):
    return lax.dot_general(
        left, right, (((left_dim,), (right_dim,)), ((), ())), preferred_element_type=f32
    )


def layer_norm(values, gain, shift):
    row_mean = jnp.mean(values, axis=-1, keepdims=True)
    centered = values - row_mean
    inverse = lax.rsqrt(jnp.mean(centered * centered, axis=-1, keepdims=True) + norm_eps)
    normed = centered * inverse
    return (normed * gain + shift, normed, inverse)


def norm_back(grad_norm, normed, inverse, gain):
    scaled = grad_norm * gain
    grad_input = inverse * (
        scaled
        - jnp.mean(scaled, axis=-1, keepdims=True)
        - normed * jnp.mean(scaled * normed, axis=-1, keepdims=True)
    )
    return (grad_input, jnp.sum(grad_norm * normed, axis=0), jnp.sum(grad_norm, axis=0))


def sweep_forward(live_views, q_pad, kv, v_ones, carry, last):
    count = q_pad.shape[1]
    keys = kv.shape[0]
    sum_rows = v_ones.shape[0]
    bq, bk = 2048, 512

    def kernel(*refs):
        live_ref, q_ref, kv_ref, v_ref = refs[:4]
        refs = refs[4:]
        if carry is not None:
            start = (refs[0][...], refs[1][...])
            refs = refs[2:]
        else:
            start = (jnp.full((1, bq), -1e30, f32), jnp.zeros((sum_rows, bq), f32))
        queries = q_ref[...]

        def view_step(view, running):
            top, accum = running
            for part in range(VIEW_TOK // bk):
                first = pl.multiple_of(view * VIEW_TOK + part * bk, bk)
                scores = dot(kv_ref[pl.ds(first, bk), :], queries)
                new_top = jnp.maximum(top, jnp.max(scores, axis=0, keepdims=True))
                weights = jnp.exp2(scores - new_top).astype(bf16)
                accum = accum * jnp.exp2(top - new_top) + dot(v_ref[:, pl.ds(first, bk)], weights)
                top = new_top
            return (top, accum)

        top, accum = lax.fori_loop(0, live_ref[0], view_step, start)
        if last:
            total = accum[HEAD_DIM : HEAD_DIM + 1]
            heads_out = accum[:HEAD_DIM] / total
            refs[0][...] = heads_out
            refs[1][...] = heads_out.astype(bf16)
            refs[2][...] = top + jnp.log2(total)
        else:
            refs[0][...] = top
            refs[1][...] = accum

    def columns(rows):
        return pl.BlockSpec((rows, bq), lambda i: (0, i))

    whole = [
        pl.BlockSpec((keys, kv.shape[1]), lambda i: (0, 0)),
        pl.BlockSpec((sum_rows, keys), lambda i: (0, 0)),
    ]
    in_specs = [pl.BlockSpec(memory_space=pltpu.SMEM), columns(q_pad.shape[0])] + whole
    operands = [live_views, q_pad, kv, v_ones]
    if carry is not None:
        in_specs += [columns(1), columns(sum_rows)]
        operands += list(carry)
    if last:
        shapes = [((HEAD_DIM, count), f32), ((HEAD_DIM, count), bf16), ((1, count), f32)]
    else:
        shapes = [((1, count), f32), ((sum_rows, count), f32)]
    return pl.pallas_call(
        kernel,
        grid=(count // bq,),
        in_specs=in_specs,
        out_specs=[columns(shape[0]) for shape, _ in shapes],
        out_shape=[jax.ShapeDtypeStruct(shape, kind) for shape, kind in shapes],
        compiler_params=pltpu.CompilerParams(vmem_limit_bytes=VMEM_BYTES),
        cost_estimate=pl.CostEstimate(
            flops=16 * HEAD_DIM * count * keys, bytes_accessed=8 << 20, transcendentals=count * keys
        ),
    )(*operands)


def sweep_backward(live_views, q_pad, g_pad, q_rows, g_rows, kv, k_cols, log_norm, delta, carry):
    count = q_pad.shape[1]
    keys = kv.shape[0]
    bq, bk = 1024, 512
    last = carry is not None

    def kernel(*refs):
        live_ref, q_ref, g_ref, qr_ref, gr_ref, kv_ref, kc_ref, norm_ref, delta_ref = refs[:9]
        carry_ref = refs[9] if last else None
        pairs_ref, out_ref, total_ref = refs[-3:]
        step = pl.program_id(0)

        @pl.when(step == 0)
        def _():
            total_ref[...] = carry_ref[...] if last else jnp.zeros_like(total_ref)

        live = step * bk < live_ref[0] * VIEW_TOK

        @pl.when(live)
        def _():
            key_values = kv_ref[...]
            key_columns = kc_ref[...]
            accum = jnp.zeros((bk, 2 * HEAD_DIM), f32)
            for part in range(count // bq):
                span = pl.ds(part * bq, bq)
                scores = dot(key_values, q_ref[:, span])
                weights = jnp.exp2(scores - norm_ref[:, span])
                grad_weights = dot(key_values, g_ref[:, span])
                grad_scores = (weights * (grad_weights - delta_ref[:, span])).astype(bf16)
                accum += dot(weights.astype(bf16), gr_ref[span, :])
                accum += dot(grad_scores, qr_ref[span, :])
                total_ref[:, span] += dot(key_columns, grad_scores)
            lane = lax.broadcasted_iota(jnp.int32, accum.shape, 1)
            pairs_ref[...] = jnp.where(lane < HEAD_DIM, accum * (1.0 / LOG2E), accum).astype(bf16)

        @pl.when(jnp.logical_not(live))
        def _():
            pairs_ref[...] = jnp.zeros_like(pairs_ref)

        @pl.when(step == pl.num_programs(0) - 1)
        def _():
            if last:
                out_ref[...] = (total_ref[...] * HEAD_DIM ** (-0.5)).astype(bf16)
            else:
                out_ref[...] = total_ref[...]

    def whole(array):
        return pl.BlockSpec(array.shape, lambda i: (0, 0))

    in_specs = [
        pl.BlockSpec(memory_space=pltpu.SMEM),
        whole(q_pad),
        whole(g_pad),
        whole(q_rows),
        whole(g_rows),
        pl.BlockSpec((bk, 2 * HEAD_DIM), lambda i: (i, 0)),
        pl.BlockSpec((HEAD_DIM, bk), lambda i: (0, i)),
        whole(log_norm),
        whole(delta),
    ]
    operands = [live_views, q_pad, g_pad, q_rows, g_rows, kv, k_cols, log_norm, delta]
    if last:
        in_specs.append(whole(carry))
        operands.append(carry)
    return pl.pallas_call(
        kernel,
        grid=(keys // bk,),
        in_specs=in_specs,
        out_specs=[
            pl.BlockSpec((bk, 2 * HEAD_DIM), lambda i: (i, 0)),
            pl.BlockSpec((HEAD_DIM, count), lambda i: (0, 0)),
        ],
        out_shape=[
            jax.ShapeDtypeStruct((keys, 2 * HEAD_DIM), bf16),
            jax.ShapeDtypeStruct((HEAD_DIM, count), bf16 if last else f32),
        ],
        scratch_shapes=[pltpu.VMEM((HEAD_DIM, count), f32)],
        compiler_params=pltpu.CompilerParams(vmem_limit_bytes=VMEM_BYTES),
        cost_estimate=pl.CostEstimate(
            flops=40 * HEAD_DIM * count * keys, bytes_accessed=10 << 20, transcendentals=count * keys
        ),
    )(*operands)


MESH = pl.DeviceIdType.MESH


def greet(peers):
    barrier = pltpu.get_barrier_semaphore()
    for peer in peers:
        pl.semaphore_signal(barrier, inc=1, device_id=peer, device_id_type=MESH)
    pl.semaphore_wait(barrier, len(peers))


def window(start, size, axis):
    span = pl.ds(pl.multiple_of(start, size), size)
    return (span, slice(None)) if axis == 0 else (slice(None), span)


def exchange(number, ways, *items):
    def kernel(*refs):
        count = len(items)
        sources, targets = refs[:count], refs[count : 2 * count]
        own_sems, send_sems, recv_sems = refs[2 * count :]
        position = lax.axis_index("dp")
        place = position % (2 * ways) // 2
        base = position - 2 * place
        places = [lax.rem(place + distance, ways) for distance in range(ways)]
        greet([{"dp": base + 2 * places[distance]} for distance in range(1, ways)])
        copies = []
        for distance in range(1, ways):
            for index, (array, split, concat) in enumerate(items):
                size = array.shape[split] // ways
                copy = pltpu.make_async_remote_copy(
                    src_ref=sources[index].at[window(places[distance] * size, size, split)],
                    dst_ref=targets[index].at[
                        window(place * array.shape[concat], array.shape[concat], concat)
                    ],
                    send_sem=send_sems.at[index, distance],
                    recv_sem=recv_sems.at[index, distance],
                    device_id={"dp": base + 2 * places[distance]},
                    device_id_type=MESH,
                )
                copy.start()
                copies.append(copy)
        for index, (array, split, concat) in enumerate(items):
            size = array.shape[split] // ways
            copy = pltpu.make_async_copy(
                sources[index].at[window(place * size, size, split)],
                targets[index].at[
                    window(place * array.shape[concat], array.shape[concat], concat)
                ],
                own_sems.at[index],
            )
            copy.start()
            copies.append(copy)
        for copy in copies:
            copy.wait()

    def shape(array, split, concat):
        sizes = list(array.shape)
        sizes[split] //= ways
        sizes[concat] *= ways
        return jax.ShapeDtypeStruct(tuple(sizes), array.dtype)

    count = len(items)
    vmem = pl.BlockSpec(memory_space=pltpu.VMEM)
    moved = sum(array.size * array.dtype.itemsize for array, _, _ in items)
    return pl.pallas_call(
        kernel,
        in_specs=[vmem] * count,
        out_specs=[vmem] * count,
        out_shape=[shape(*item) for item in items],
        scratch_shapes=[
            pltpu.SemaphoreType.DMA((count,)),
            pltpu.SemaphoreType.DMA((count, ways)),
            pltpu.SemaphoreType.DMA((count, ways)),
        ],
        compiler_params=pltpu.CompilerParams(
            collective_id=number, has_side_effects=True, vmem_limit_bytes=16 << 20
        ),
        cost_estimate=pl.CostEstimate(flops=0, bytes_accessed=40 * moved, transcendentals=0),
    )(*[array for array, _, _ in items])


def last_sums(number, ways, grads, far_part, own_part, small):
    chunks = []
    for index, grad in enumerate(grads):
        for first in range(0, grad.shape[0], max(grad.shape[0] * (256 << 10) // grad.size, 1)):
            chunks.append((index, first, max(grad.shape[0] * (256 << 10) // grad.size, 1)))
    lots = len(chunks)
    rounds = 5

    def kernel(*refs):
        count = len(grads)
        sources = refs[:count]
        far_ref, own_ref, small_ref = refs[count : count + 3]
        results = refs[count + 3 : 2 * count + 3]
        sum_ref, small_sum_ref = refs[2 * count + 3 : 2 * count + 5]
        refs = refs[2 * count + 5 :]
        x_in, x_sums, z_in = refs[:lots], refs[lots : 2 * lots], refs[2 * lots : 3 * lots]
        core_in, pair_ref, chip_in, small_in, small_out = refs[3 * lots : 3 * lots + 5]
        sems = refs[3 * lots + 5 :]
        position = lax.axis_index("dp")
        slot = lax.axis_index("tensor")
        place = position % (2 * ways) // 2
        side = position % 2
        base = position - 2 * place
        across = {"dp": position + 1 - 2 * side}
        places = [lax.rem(place + distance, ways) for distance in range(ways)]
        peers = [{"dp": base + 2 * at} for at in places]
        partner = slot + 1 - 2 * lax.rem(slot, 2)
        chip = lax.rem(slot + 2, 4)
        core_to, chip_to = {"tensor": partner}, {"tensor": chip}
        even = place + 1 - 2 * lax.rem(place, 2)
        steps = [
            core_to,
            chip_to,
            across,
            {"dp": base + 2 * even},
            {"dp": base + 2 * lax.rem(place + 2, ways)},
        ]
        greet([across, core_to, chip_to] + peers[1:])
        pending = []

        def send(source, target, pair, at, to):
            copy = pltpu.make_async_remote_copy(
                src_ref=source,
                dst_ref=target,
                send_sem=sems[2 * pair].at[at],
                recv_sem=sems[2 * pair + 1].at[at],
                device_id=to,
                device_id_type=MESH,
            )
            copy.start()
            pending.append(copy)
            return copy

        core_copy = send(far_ref, core_in, 0, 0, core_to)
        small_copy = send(small_ref, small_in.at[0], 1, 0, steps[0])
        across_copies = []
        for lot, (index, first, rows) in enumerate(chunks):
            half = rows // 2
            given = window(first + (1 - side) * half, half, 0)
            across_copies.append(send(sources[index].at[given], x_in[lot], 2, lot, across))

        def small_round(at, copy):
            copy.wait_recv()
            total = (small_ref if at == 0 else small_out.at[at - 1])[...] + small_in[at]
            if at == rounds - 1:
                small_sum_ref[...] = total
                return None
            small_out[at] = total
            return send(small_out.at[at], small_in.at[at + 1], 1, at + 1, steps[at + 1])

        def reduce_across(lot):
            index, first, rows = chunks[lot]
            half, part = rows // 2, rows // 2 // ways
            across_copies[lot].wait_recv()
            kept = sources[index][window(first + side * half, half, 0)]
            x_sums[lot][...] = (kept.astype(f32) + x_in[lot][...].astype(f32)).astype(bf16)
            return [
                send(
                    x_sums[lot].at[window(places[distance] * part, part, 0)],
                    z_in[lot].at[distance - 1],
                    3,
                    lot * ways + distance,
                    peers[distance],
                )
                for distance in range(1, ways)
            ]

        def reduce_places(lot, copies):
            index, first, rows = chunks[lot]
            half, part = rows // 2, rows // 2 // ways
            total = x_sums[lot][window(place * part, part, 0)].astype(f32)
            for distance in range(1, ways):
                copies[distance - 1].wait_recv()
                total += z_in[lot][distance - 1].astype(f32)
            mine = window(first + side * half + place * part, part, 0)
            results[index][mine] = total.astype(bf16)
            return [
                send(
                    results[index].at[mine],
                    results[index].at[mine],
                    4,
                    lot * ways + distance,
                    peers[distance],
                )
                for distance in range(1, ways)
            ]

        def give_across(lot, copies):
            index, first, rows = chunks[lot]
            half = rows // 2
            for copy in copies:
                copy.wait_recv()
            mine = window(first + side * half, half, 0)
            return send(results[index].at[mine], results[index].at[mine], 5, lot, across)

        core_copy.wait_recv()
        pair_ref[...] = (own_ref[...] + core_in[...].astype(f32)).astype(bf16)
        chip_copy = send(pair_ref, chip_in, 6, 0, chip_to)
        small_copy = small_round(0, small_copy)
        reduced, gathered, given = {}, {}, {}
        for step in range(lots + 3):
            if step < lots:
                reduced[step] = reduce_across(step)
            if 1 <= step < lots + 1:
                gathered[step - 1] = reduce_places(step - 1, reduced[step - 1])
            if 2 <= step < lots + 2:
                given[step - 2] = give_across(step - 2, gathered[step - 2])
            if 1 <= step + 1 < rounds:
                small_copy = small_round(step + 1, small_copy)
        chip_copy.wait_recv()
        sum_ref[...] = pair_ref[...].astype(f32) + chip_in[...].astype(f32)
        for lot in range(lots):
            given[lot].wait_recv()
        for copy in pending:
            copy.wait_send()

    vmem = pl.BlockSpec(memory_space=pltpu.VMEM)
    shapes = [jax.ShapeDtypeStruct(grad.shape, bf16) for grad in grads]
    shapes += [jax.ShapeDtypeStruct(own_part.shape, f32), jax.ShapeDtypeStruct(small.shape, f32)]
    wide = [grads[index].shape[1] for index, _, _ in chunks]
    scratch = [pltpu.VMEM((lot[2] // 2, w), bf16) for lot, w in zip(chunks, wide)]
    scratch += [pltpu.VMEM((lot[2] // 2, w), bf16) for lot, w in zip(chunks, wide)]
    scratch += [pltpu.VMEM((ways - 1, lot[2] // 2 // ways, w), bf16) for lot, w in zip(chunks, wide)]
    scratch += [pltpu.VMEM(far_part.shape, bf16)] * 3
    scratch += [pltpu.VMEM((rounds,) + small.shape, f32)] * 2
    for number_of in (1, rounds, lots, lots * ways, lots * ways, lots, 1):
        scratch += [pltpu.SemaphoreType.DMA((number_of,))] * 2
    return pl.pallas_call(
        kernel,
        in_specs=[vmem] * (len(grads) + 3),
        out_specs=[vmem] * len(shapes),
        out_shape=shapes,
        scratch_shapes=scratch,
        compiler_params=pltpu.CompilerParams(
            collective_id=number, has_side_effects=True, vmem_limit_bytes=32 << 20
        ),
        cost_estimate=pl.CostEstimate(flops=0, bytes_accessed=150 << 20, transcendentals=0),
    )(*grads, far_part, own_part, small)


def shards(
    tokens,
    views,
    ln1_gain,
    ln1_bias,
    w_query,
    w_key,
    w_value,
    w_out,
    ln2_gain,
    ln2_bias,
    w_up,
    w_down,
    cotangent,
):
    row_count, width = tokens.shape
    inner = w_query.shape[1]
    heads = inner // HEAD_DIM
    half = row_count // 2
    group = MAX_VIEWS * VIEW_TOK // row_count
    devices = lax.axis_size("dp")
    assert row_count == VIEW_TOK and group == 2 * heads and lax.axis_size("tensor") == 4
    position = lax.axis_index("dp")
    block = position % group
    side = block % 2
    core = lax.axis_index("tensor") % 2
    scene_views = lax.dynamic_index_in_dim(views, position // group, keepdims=False)
    own_views = ((scene_views + 1 - side) // 2).reshape(1)
    far_views = ((scene_views + side) // 2).reshape(1)
    keep = (block < scene_views).astype(f32)
    def across(block):
        return lax.ppermute(block, "dp", [(i, i ^ 1) for i in range(devices)])

    def other_core(block):
        return lax.ppermute(block, "tensor", [(i, i ^ 1) for i in range(4)])

    def other_chip(block):
        return lax.ppermute(block, "tensor", [(i, i ^ 2) for i in range(4)])

    def own_first(block):
        return jnp.where(core == 0, block, jnp.concatenate([block[half:], block[:half]], axis=0))

    def pair_sum(far_part, own_part):
        arrived = other_core(far_part.astype(bf16))
        return (own_part + arrived.astype(f32)).astype(bf16)

    def both_halves(own):
        return jnp.concatenate([own, other_core(own)], axis=0)

    rows = own_first(tokens)
    grad_rows = own_first(cotangent)
    inputs_own = rows[:half].astype(f32)
    grad_own = grad_rows[:half].astype(f32)

    attn_norm, normed_first, inverse_first = layer_norm(rows.astype(f32), ln1_gain, ln1_bias)
    attn_in = attn_norm.astype(bf16)
    w_pairs = jnp.concatenate(
        [w_key.reshape(width, heads, HEAD_DIM), w_value.reshape(width, heads, HEAD_DIM)], axis=2
    ).reshape(width, 2 * inner)
    kv_low = dot(attn_in, w_pairs).astype(bf16)
    query_low = (contract(w_query, attn_in, 0, 1) * (LOG2E * HEAD_DIM ** (-0.5))).astype(bf16)
    q_cols, kv_own = exchange(1, heads, (query_low, 0, 1), (kv_low, 1, 0))
    kv_far = across(kv_own)

    empty = jnp.zeros_like(q_cols)
    q_pad = jnp.concatenate([q_cols, empty], axis=0)

    def value_columns(kv):
        cols = kv.T
        ones = jnp.ones((16, cols.shape[1]), bf16)
        return cols[:HEAD_DIM], jnp.concatenate([cols[HEAD_DIM:], ones], axis=0)

    k_own, v_own = value_columns(kv_own)
    carry = sweep_forward(own_views, q_pad, kv_own, v_own, None, False)
    k_far, v_far = value_columns(kv_far)
    heads_out, heads_low, log_norm = sweep_forward(far_views, q_pad, kv_far, v_far, carry, True)
    (attn_cols,) = exchange(2, heads, (heads_low, 1, 0))

    pair = pair_sum(
        contract(attn_cols[:, half:], w_out, 0, 0), contract(attn_cols[:, :half], w_out, 0, 0)
    )
    resid = inputs_own + keep * (pair.astype(f32) + other_chip(pair).astype(f32))
    mlp_norm, normed_second, inverse_second = layer_norm(resid, ln2_gain, ln2_bias)
    mlp_in = both_halves(mlp_norm.astype(bf16))
    grad_mlp = (keep * grad_rows.astype(f32)).astype(bf16)
    grad_act = lax.optimization_barrier(contract(grad_mlp, w_down, 1, 1))
    up_proj = dot(mlp_in, w_up)
    activated, gelu_pull = jax.vjp(partial(jax.nn.gelu, approximate=True), up_proj)
    act_low = activated.astype(bf16)
    grad_up = gelu_pull(grad_act)[0].astype(bf16)
    pair = pair_sum(contract(grad_up[half:], w_up, 1, 1), contract(grad_up[:half], w_up, 1, 1))
    w_down_grad = contract(act_low, grad_mlp, 0, 0).astype(bf16)
    w_up_grad = contract(mlp_in, grad_up, 0, 0).astype(bf16)
    arrived, act_low, w_up_grad, w_down_grad = lax.optimization_barrier(
        (other_chip(pair), act_low, w_up_grad, w_down_grad)
    )
    early = lax.psum((w_up_grad, w_down_grad), "dp")
    grad_mlp_in = pair.astype(f32) + arrived.astype(f32)
    mlp_pair = pair_sum(dot(act_low[half:], w_down), dot(act_low[:half], w_down))
    mlp_arrived = other_chip(mlp_pair)
    grad_second, ln2_gain_grad, ln2_bias_grad = norm_back(
        grad_mlp_in, normed_second, inverse_second, ln2_gain
    )
    grad_resid = grad_own + grad_second
    grad_attn = both_halves((keep * grad_resid).astype(bf16))
    grad_heads = contract(w_out, grad_attn, 1, 1).astype(bf16)
    (g_cols,) = exchange(3, heads, (grad_heads, 0, 1))
    w_out_grad = dot(attn_cols, grad_attn).astype(bf16)

    g_pad = jnp.concatenate([empty, g_cols], axis=0)
    delta = jnp.sum(g_cols.astype(f32) * heads_out, axis=0, keepdims=True)
    q_rows = q_pad.T
    g_rows = g_pad.T
    pairs_far, carry = sweep_backward(
        far_views, q_pad, g_pad, q_rows, g_rows, kv_far, k_far, log_norm, delta, None
    )
    resid, mlp_pair, mlp_arrived, pairs_far = lax.optimization_barrier(
        (resid, mlp_pair, mlp_arrived, pairs_far)
    )
    mixed_own = (
        resid + keep * (mlp_pair.astype(f32) + mlp_arrived.astype(f32))
    ).astype(bf16)
    arrived = across(pairs_far)
    pairs_own, dq_cols = sweep_backward(
        own_views, q_pad, g_pad, q_rows, g_rows, kv_own, k_own, log_norm, delta, carry
    )
    pairs = (pairs_own.astype(f32) + arrived.astype(f32)).astype(bf16)
    grad_query, grad_pairs = exchange(4, heads, (dq_cols, 1, 0), (pairs, 0, 1))

    def partial_in(start):
        return contract(grad_query[:, start : start + half], w_query, 0, 1) + contract(
            grad_pairs[start : start + half], w_pairs, 1, 1
        )

    far_part, own_part = partial_in(half), partial_in(0)
    small = jnp.stack(
        [
            jnp.sum(far_part * normed_first[half:], axis=0)
            + jnp.sum(own_part * normed_first[:half], axis=0),
            jnp.sum(far_part, axis=0) + jnp.sum(own_part, axis=0),
            ln2_gain_grad * 0.5,
            ln2_bias_grad * 0.5,
        ]
        + [jnp.zeros((width,), f32)] * 4
    )
    late = (
        w_out_grad,
        contract(attn_in, grad_pairs, 0, 0).astype(bf16),
        contract(attn_in, grad_query, 0, 1).astype(bf16),
    )
    w_out_grad, w_pairs_grad, w_query_grad, grad_attn_in, small = last_sums(
        5, heads, late, far_part.astype(bf16), own_part, small
    )
    if devices > group:
        same = [list(range(at, devices, group)) for at in range(group)]
        w_out_grad, w_pairs_grad, w_query_grad, small = [
            lax.psum(array, "dp", axis_index_groups=same)
            for array in (w_out_grad, w_pairs_grad, w_query_grad, small)
        ]
    grad_first, _, _ = norm_back(
        grad_attn_in, normed_first[:half], inverse_first[:half], ln1_gain
    )
    tokens_grad_own = (grad_resid + grad_first).astype(bf16)
    w_pairs_grad = w_pairs_grad.astype(f32).reshape(width, heads, 2 * HEAD_DIM)

    def in_order(own):
        far = other_core(own)
        return jnp.where(
            core == 0, jnp.concatenate([own, far], axis=0), jnp.concatenate([far, own], axis=0)
        )

    return (
        in_order(mixed_own),
        in_order(tokens_grad_own),
        small[0],
        small[1],
        w_query_grad.astype(f32),
        w_pairs_grad[:, :, :HEAD_DIM].reshape(width, inner),
        w_pairs_grad[:, :, HEAD_DIM:].reshape(width, inner),
        w_out_grad.astype(f32),
        small[2],
        small[3],
        early[0].astype(f32),
        early[1].astype(f32),
    )


def solution(mesh):
    placed = (
        P("dp", None),
        P(),
        P(),
        P(),
        P(None, "tensor"),
        P(None, "tensor"),
        P(None, "tensor"),
        P("tensor", None),
        P(),
        P(),
        P(None, "tensor"),
        P("tensor", None),
        P("dp", None),
    )
    return jax.shard_map(
        shards,
        mesh=mesh,
        in_specs=placed,
        out_specs=(
            P("dp", None),
            P("dp", None),
            P(),
            P(),
            P(None, "tensor"),
            P(None, "tensor"),
            P(None, "tensor"),
            P("tensor", None),
            P(),
            P(),
            P(None, "tensor"),
            P("tensor", None),
        ),
        check_vma=False,
    )
```

```python
from functools import partial
import math

import jax
import jax.numpy as jnp
from jax import lax
from jax.experimental import pallas as pl
from jax.experimental.pallas import tpu as pltpu
from jax.sharding import PartitionSpec as P

HEAD_DIM = 64
VIEW_TOK = 1024
MAX_VIEWS = 8
LOG2E = math.log2(math.e)
VMEM_BYTES = 48 << 20
LOT = 128 << 10

norm_eps = 1e-05

bf16 = jnp.bfloat16
f32 = jnp.float32
dot = partial(jnp.dot, preferred_element_type=f32)


def contract(left, right, left_dim, right_dim):
    return lax.dot_general(
        left, right, (((left_dim,), (right_dim,)), ((), ())), preferred_element_type=f32
    )


def layer_norm(values, gain, shift):
    row_mean = jnp.mean(values, axis=-1, keepdims=True)
    centered = values - row_mean
    inverse = lax.rsqrt(jnp.mean(centered * centered, axis=-1, keepdims=True) + norm_eps)
    normed = centered * inverse
    return (normed * gain + shift, normed, inverse)


def norm_back(grad_norm, normed, inverse, gain):
    scaled = grad_norm * gain
    grad_input = inverse * (
        scaled
        - jnp.mean(scaled, axis=-1, keepdims=True)
        - normed * jnp.mean(scaled * normed, axis=-1, keepdims=True)
    )
    return (grad_input, jnp.sum(grad_norm * normed, axis=0), jnp.sum(grad_norm, axis=0))


def sweep_forward(live_views, q_cols, kv, carry, last):
    count = q_cols.shape[1]
    keys = kv.shape[0]
    sum_rows = HEAD_DIM + 16
    bq, bk = 2048, 512

    def kernel(*refs):
        live_ref, q_ref, kv_ref = refs[:3]
        columns_ref = refs[-1]
        refs = refs[3:-1]
        if carry is not None:
            start = (refs[0][...], refs[1][...])
            refs = refs[2:]
        else:
            start = (jnp.full((1, bq), -1e30, f32), jnp.zeros((sum_rows, bq), f32))
        queries = jnp.concatenate([q_ref[...], jnp.zeros((HEAD_DIM, bq), bf16)], axis=0)

        @pl.when(pl.program_id(0) == 0)
        def _():
            columns_ref[HEAD_DIM:, :] = jnp.ones((16, keys), bf16)
            columns_ref[:HEAD_DIM, :] = kv_ref[...].T[HEAD_DIM:]

        def view_step(view, running):
            top, accum = running
            for part in range(VIEW_TOK // bk):
                first = pl.multiple_of(view * VIEW_TOK + part * bk, bk)
                scores = dot(kv_ref[pl.ds(first, bk), :], queries)
                new_top = jnp.maximum(top, jnp.max(scores, axis=0, keepdims=True))
                weights = jnp.exp2(scores - new_top).astype(bf16)
                accum = accum * jnp.exp2(top - new_top) + dot(
                    columns_ref[:, pl.ds(first, bk)], weights
                )
                top = new_top
            return (top, accum)

        top, accum = lax.fori_loop(0, live_ref[0], view_step, start)
        if last:
            total = accum[HEAD_DIM : HEAD_DIM + 1]
            heads_out = accum[:HEAD_DIM] / total
            refs[0][...] = heads_out
            refs[1][...] = heads_out.astype(bf16)
            refs[2][...] = top + jnp.log2(total)
        else:
            refs[0][...] = top
            refs[1][...] = accum

    def columns(rows):
        return pl.BlockSpec((rows, bq), lambda i: (0, i))

    in_specs = [
        pl.BlockSpec(memory_space=pltpu.SMEM),
        columns(HEAD_DIM),
        pl.BlockSpec(kv.shape, lambda i: (0, 0)),
    ]
    operands = [live_views, q_cols, kv]
    if carry is not None:
        in_specs += [columns(1), columns(sum_rows)]
        operands += list(carry)
    if last:
        shapes = [((HEAD_DIM, count), f32), ((HEAD_DIM, count), bf16), ((1, count), f32)]
    else:
        shapes = [((1, count), f32), ((sum_rows, count), f32)]
    return pl.pallas_call(
        kernel,
        grid=(count // bq,),
        in_specs=in_specs,
        out_specs=[columns(shape[0]) for shape, _ in shapes],
        out_shape=[jax.ShapeDtypeStruct(shape, kind) for shape, kind in shapes],
        scratch_shapes=[pltpu.VMEM((sum_rows, keys), bf16)],
        compiler_params=pltpu.CompilerParams(vmem_limit_bytes=VMEM_BYTES),
        cost_estimate=pl.CostEstimate(
            flops=16 * HEAD_DIM * count * keys, bytes_accessed=8 << 20, transcendentals=count * keys
        ),
    )(*operands)


def sweep_backward(live_views, q_cols, g_cols, heads_out, kv, log_norm, carry):
    count = q_cols.shape[1]
    keys = kv.shape[0]
    bq, bk = 1024, 512
    last = carry is not None

    def kernel(*refs):
        live_ref, q_ref, g_ref, heads_ref, kv_ref, norm_ref = refs[:6]
        carry_ref = refs[6] if last else None
        pairs_ref, out_ref, total_ref, rows_ref, delta_ref = refs[-5:]
        step = pl.program_id(0)

        @pl.when(step == 0)
        def _():
            total_ref[...] = carry_ref[...] if last else jnp.zeros_like(total_ref)
            rows_ref[...] = jnp.concatenate([q_ref[...], g_ref[...]], axis=0).T
            delta_ref[...] = jnp.sum(
                g_ref[...].astype(f32) * heads_ref[...], axis=0, keepdims=True
            )

        live = step * bk < live_ref[0] * VIEW_TOK

        @pl.when(live)
        def _():
            key_values = kv_ref[...]
            key_columns = key_values.T[:HEAD_DIM]
            empty = jnp.zeros((HEAD_DIM, bq), bf16)
            is_key = lax.broadcasted_iota(jnp.int32, (bq, 2 * HEAD_DIM), 1) < HEAD_DIM

            def parts(pair, accum):
                for bit in range(2):
                    span = pl.ds(pl.multiple_of((pair * 2 + bit) * bq, bq), bq)
                    scores = dot(key_values, jnp.concatenate([q_ref[:, span], empty], axis=0))
                    weights = jnp.exp2(scores - norm_ref[:, span])
                    grad_weights = dot(
                        key_values, jnp.concatenate([empty, g_ref[:, span]], axis=0)
                    )
                    grad_scores = (weights * (grad_weights - delta_ref[:, span])).astype(bf16)
                    rows = rows_ref[span, :]
                    none = jnp.zeros_like(rows)
                    accum += dot(weights.astype(bf16), jnp.where(is_key, none, rows))
                    accum += dot(grad_scores, jnp.where(is_key, rows, none))
                    total_ref[:, span] += dot(key_columns, grad_scores)
                return accum

            accum = lax.fori_loop(
                0, count // (2 * bq), parts, jnp.zeros((bk, 2 * HEAD_DIM), f32)
            )
            lane = lax.broadcasted_iota(jnp.int32, accum.shape, 1)
            pairs_ref[...] = jnp.where(lane < HEAD_DIM, accum * (1.0 / LOG2E), accum).astype(bf16)

        @pl.when(jnp.logical_not(live))
        def _():
            pairs_ref[...] = jnp.zeros_like(pairs_ref)

        @pl.when(step == pl.num_programs(0) - 1)
        def _():
            if last:
                out_ref[...] = (total_ref[...] * HEAD_DIM ** (-0.5)).astype(bf16)
            else:
                out_ref[...] = total_ref[...]

    def whole(array):
        return pl.BlockSpec(array.shape, lambda i: (0, 0))

    by_keys = pl.BlockSpec((bk, 2 * HEAD_DIM), lambda i: (i, 0))
    in_specs = [
        pl.BlockSpec(memory_space=pltpu.SMEM),
        whole(q_cols),
        whole(g_cols),
        whole(heads_out),
        by_keys,
        whole(log_norm),
    ]
    operands = [live_views, q_cols, g_cols, heads_out, kv, log_norm]
    if last:
        in_specs.append(whole(carry))
        operands.append(carry)
    return pl.pallas_call(
        kernel,
        grid=(keys // bk,),
        in_specs=in_specs,
        out_specs=[by_keys, pl.BlockSpec((HEAD_DIM, count), lambda i: (0, 0))],
        out_shape=[
            jax.ShapeDtypeStruct((keys, 2 * HEAD_DIM), bf16),
            jax.ShapeDtypeStruct((HEAD_DIM, count), bf16 if last else f32),
        ],
        scratch_shapes=[
            pltpu.VMEM((HEAD_DIM, count), f32),
            pltpu.VMEM((count, 2 * HEAD_DIM), bf16),
            pltpu.VMEM((1, count), f32),
        ],
        compiler_params=pltpu.CompilerParams(vmem_limit_bytes=VMEM_BYTES),
        cost_estimate=pl.CostEstimate(
            flops=40 * HEAD_DIM * count * keys, bytes_accessed=10 << 20, transcendentals=count * keys
        ),
    )(*operands)


MESH = pl.DeviceIdType.MESH


def greet(peers):
    barrier = pltpu.get_barrier_semaphore()
    for peer in peers:
        pl.semaphore_signal(barrier, inc=1, device_id=peer, device_id_type=MESH)
    pl.semaphore_wait(barrier, len(peers))


def window(start, size, axis):
    span = pl.ds(pl.multiple_of(start, size), size)
    return (span, slice(None)) if axis == 0 else (slice(None), span)


def exchange(number, ways, *items):
    def kernel(*refs):
        count = len(items)
        sources, targets = refs[:count], refs[count : 2 * count]
        own_sems, send_sems, recv_sems = refs[2 * count :]
        position = lax.axis_index("dp")
        place = position % (2 * ways) // 2
        base = position - 2 * place
        places = [lax.rem(place + distance, ways) for distance in range(ways)]
        greet([{"dp": base + 2 * places[distance]} for distance in range(1, ways)])
        copies = []
        for distance in range(1, ways):
            for index, (array, split, concat) in enumerate(items):
                size = array.shape[split] // ways
                copy = pltpu.make_async_remote_copy(
                    src_ref=sources[index].at[window(places[distance] * size, size, split)],
                    dst_ref=targets[index].at[
                        window(place * array.shape[concat], array.shape[concat], concat)
                    ],
                    send_sem=send_sems.at[index, distance],
                    recv_sem=recv_sems.at[index, distance],
                    device_id={"dp": base + 2 * places[distance]},
                    device_id_type=MESH,
                )
                copy.start()
                copies.append(copy)
        for index, (array, split, concat) in enumerate(items):
            size = array.shape[split] // ways
            copy = pltpu.make_async_copy(
                sources[index].at[window(place * size, size, split)],
                targets[index].at[
                    window(place * array.shape[concat], array.shape[concat], concat)
                ],
                own_sems.at[index],
            )
            copy.start()
            copies.append(copy)
        for copy in copies:
            copy.wait()

    def shape(array, split, concat):
        sizes = list(array.shape)
        sizes[split] //= ways
        sizes[concat] *= ways
        return jax.ShapeDtypeStruct(tuple(sizes), array.dtype)

    count = len(items)
    vmem = pl.BlockSpec(memory_space=pltpu.VMEM)
    moved = sum(array.size * array.dtype.itemsize for array, _, _ in items)
    return pl.pallas_call(
        kernel,
        in_specs=[vmem] * count,
        out_specs=[vmem] * count,
        out_shape=[shape(*item) for item in items],
        scratch_shapes=[
            pltpu.SemaphoreType.DMA((count,)),
            pltpu.SemaphoreType.DMA((count, ways)),
            pltpu.SemaphoreType.DMA((count, ways)),
        ],
        compiler_params=pltpu.CompilerParams(
            collective_id=number, has_side_effects=True, vmem_limit_bytes=16 << 20
        ),
        cost_estimate=pl.CostEstimate(flops=0, bytes_accessed=40 * moved, transcendentals=0),
    )(*[array for array, _, _ in items])


def last_sums(number, ways, grads, far_part, own_part, small):
    chunks = []
    for index, grad in enumerate(grads):
        rows = grad.shape[0] * LOT // grad.size
        chunks += [(index, first, rows) for first in range(0, grad.shape[0], rows)]
    lots = len(chunks)
    rounds = 5

    def kernel(*refs):
        count = len(grads)
        sources = refs[:count]
        far_ref, own_ref, small_ref = refs[count : count + 3]
        results = refs[count + 3 : 2 * count + 3]
        sum_ref, small_sum_ref = refs[2 * count + 3 : 2 * count + 5]
        refs = refs[2 * count + 5 :]
        x_in, x_sums, z_in = refs[:lots], refs[lots : 2 * lots], refs[2 * lots : 3 * lots]
        core_in, pair_ref, chip_in, small_in, small_out = refs[3 * lots : 3 * lots + 5]
        sems = refs[3 * lots + 5 :]
        position = lax.axis_index("dp")
        slot = lax.axis_index("tensor")
        place = position % (2 * ways) // 2
        side = position % 2
        base = position - 2 * place
        across = {"dp": position + 1 - 2 * side}
        places = [lax.rem(place + distance, ways) for distance in range(ways)]
        peers = [{"dp": base + 2 * at} for at in places]
        partner = slot + 1 - 2 * lax.rem(slot, 2)
        chip = lax.rem(slot + 2, 4)
        core_to, chip_to = {"tensor": partner}, {"tensor": chip}
        even = place + 1 - 2 * lax.rem(place, 2)
        steps = [
            core_to,
            chip_to,
            across,
            {"dp": base + 2 * even},
            {"dp": base + 2 * lax.rem(place + 2, ways)},
        ]
        greet([across, core_to, chip_to] + peers[1:])
        pending = []

        def send(source, target, pair, at, to):
            copy = pltpu.make_async_remote_copy(
                src_ref=source,
                dst_ref=target,
                send_sem=sems[2 * pair].at[at],
                recv_sem=sems[2 * pair + 1].at[at],
                device_id=to,
                device_id_type=MESH,
            )
            copy.start()
            pending.append(copy)
            return copy

        core_copy = send(far_ref, core_in, 0, 0, core_to)
        small_copy = send(small_ref, small_in.at[0], 1, 0, steps[0])
        across_copies = []
        for lot, (index, first, rows) in enumerate(chunks):
            half = rows // 2
            given = window(first + (1 - side) * half, half, 0)
            across_copies.append(send(sources[index].at[given], x_in[lot], 2, lot, across))

        def small_round(at, copy):
            copy.wait_recv()
            total = (small_ref if at == 0 else small_out.at[at - 1])[...] + small_in[at]
            if at == rounds - 1:
                small_sum_ref[...] = total
                return None
            small_out[at] = total
            return send(small_out.at[at], small_in.at[at + 1], 1, at + 1, steps[at + 1])

        def reduce_across(lot):
            index, first, rows = chunks[lot]
            half, part = rows // 2, rows // 2 // ways
            across_copies[lot].wait_recv()
            kept = sources[index][window(first + side * half, half, 0)]
            x_sums[lot][...] = (kept.astype(f32) + x_in[lot][...].astype(f32)).astype(bf16)
            return [
                send(
                    x_sums[lot].at[window(places[distance] * part, part, 0)],
                    z_in[lot].at[distance - 1],
                    3,
                    lot * ways + distance,
                    peers[distance],
                )
                for distance in range(1, ways)
            ]

        def reduce_places(lot, copies):
            index, first, rows = chunks[lot]
            half, part = rows // 2, rows // 2 // ways
            total = x_sums[lot][window(place * part, part, 0)].astype(f32)
            for distance in range(1, ways):
                copies[distance - 1].wait_recv()
                total += z_in[lot][distance - 1].astype(f32)
            mine = window(first + side * half + place * part, part, 0)
            results[index][mine] = total.astype(bf16)
            return [
                send(
                    results[index].at[mine],
                    results[index].at[mine],
                    4,
                    lot * ways + distance,
                    peers[distance],
                )
                for distance in range(1, ways)
            ]

        def give_across(lot, copies):
            index, first, rows = chunks[lot]
            half = rows // 2
            for copy in copies:
                copy.wait_recv()
            mine = window(first + side * half, half, 0)
            return send(results[index].at[mine], results[index].at[mine], 5, lot, across)

        core_copy.wait_recv()
        pair_ref[...] = (own_ref[...] + core_in[...].astype(f32)).astype(bf16)
        chip_copy = send(pair_ref, chip_in, 6, 0, chip_to)
        small_copy = small_round(0, small_copy)
        reduced, gathered, given = {}, {}, {}
        for step in range(lots + 4):
            if step < lots:
                reduced[step] = reduce_across(step)
            if 2 <= step < lots + 2:
                gathered[step - 2] = reduce_places(step - 2, reduced[step - 2])
            if step >= 4:
                given[step - 4] = give_across(step - 4, gathered[step - 4])
            if 1 <= step < rounds:
                small_copy = small_round(step, small_copy)
        chip_copy.wait_recv()
        sum_ref[...] = pair_ref[...].astype(f32) + chip_in[...].astype(f32)
        for lot in range(lots):
            given[lot].wait_recv()
        for copy in pending:
            copy.wait_send()

    vmem = pl.BlockSpec(memory_space=pltpu.VMEM)
    shapes = [jax.ShapeDtypeStruct(grad.shape, bf16) for grad in grads]
    shapes += [jax.ShapeDtypeStruct(own_part.shape, f32), jax.ShapeDtypeStruct(small.shape, f32)]
    wide = [grads[index].shape[1] for index, _, _ in chunks]
    scratch = [pltpu.VMEM((lot[2] // 2, w), bf16) for lot, w in zip(chunks, wide)]
    scratch += [pltpu.VMEM((lot[2] // 2, w), bf16) for lot, w in zip(chunks, wide)]
    scratch += [pltpu.VMEM((ways - 1, lot[2] // 2 // ways, w), bf16) for lot, w in zip(chunks, wide)]
    scratch += [pltpu.VMEM(far_part.shape, bf16)] * 3
    scratch += [pltpu.VMEM((rounds,) + small.shape, f32)] * 2
    for number_of in (1, rounds, lots, lots * ways, lots * ways, lots, 1):
        scratch += [pltpu.SemaphoreType.DMA((number_of,))] * 2
    return pl.pallas_call(
        kernel,
        in_specs=[vmem] * (len(grads) + 3),
        out_specs=[vmem] * len(shapes),
        out_shape=shapes,
        scratch_shapes=scratch,
        compiler_params=pltpu.CompilerParams(
            collective_id=number, has_side_effects=True, vmem_limit_bytes=32 << 20
        ),
        cost_estimate=pl.CostEstimate(flops=0, bytes_accessed=150 << 20, transcendentals=0),
    )(*grads, far_part, own_part, small)


def shards(
    tokens,
    views,
    ln1_gain,
    ln1_bias,
    w_query,
    w_key,
    w_value,
    w_out,
    ln2_gain,
    ln2_bias,
    w_up,
    w_down,
    cotangent,
):
    row_count, width = tokens.shape
    inner = w_query.shape[1]
    heads = inner // HEAD_DIM
    half = row_count // 2
    group = MAX_VIEWS * VIEW_TOK // row_count
    devices = lax.axis_size("dp")
    assert row_count == VIEW_TOK and group == 2 * heads and lax.axis_size("tensor") == 4
    position = lax.axis_index("dp")
    block = position % group
    side = block % 2
    core = lax.axis_index("tensor") % 2
    scene_views = lax.dynamic_index_in_dim(views, position // group, keepdims=False)
    own_views = ((scene_views + 1 - side) // 2).reshape(1)
    far_views = ((scene_views + side) // 2).reshape(1)
    keep = (block < scene_views).astype(f32)
    def across(block):
        return lax.ppermute(block, "dp", [(i, i ^ 1) for i in range(devices)])

    def other_core(block):
        return lax.ppermute(block, "tensor", [(i, i ^ 1) for i in range(4)])

    def other_chip(block):
        return lax.ppermute(block, "tensor", [(i, i ^ 2) for i in range(4)])

    def own_first(block):
        return jnp.where(core == 0, block, jnp.concatenate([block[half:], block[:half]], axis=0))

    def pair_sum(far_part, own_part):
        arrived = other_core(far_part.astype(bf16))
        return (own_part + arrived.astype(f32)).astype(bf16)

    def both_halves(own):
        return jnp.concatenate([own, other_core(own)], axis=0)

    rows = own_first(tokens)
    grad_rows = own_first(cotangent)
    inputs_own = rows[:half].astype(f32)
    grad_own = grad_rows[:half].astype(f32)

    attn_norm, normed_first, inverse_first = layer_norm(rows.astype(f32), ln1_gain, ln1_bias)
    attn_in = attn_norm.astype(bf16)
    w_pairs = jnp.concatenate(
        [w_key.reshape(width, heads, HEAD_DIM), w_value.reshape(width, heads, HEAD_DIM)], axis=2
    ).reshape(width, 2 * inner)
    kv_low = dot(attn_in, w_pairs).astype(bf16)
    query_low = (contract(w_query, attn_in, 0, 1) * (LOG2E * HEAD_DIM ** (-0.5))).astype(bf16)
    q_cols, kv_own = exchange(1, heads, (query_low, 0, 1), (kv_low, 1, 0))
    kv_far = across(kv_own)

    carry = sweep_forward(own_views, q_cols, kv_own, None, False)
    heads_out, heads_low, log_norm = sweep_forward(far_views, q_cols, kv_far, carry, True)
    (attn_cols,) = exchange(2, heads, (heads_low, 1, 0))

    pair = pair_sum(
        contract(attn_cols[:, half:], w_out, 0, 0), contract(attn_cols[:, :half], w_out, 0, 0)
    )
    resid = inputs_own + keep * (pair.astype(f32) + other_chip(pair).astype(f32))
    mlp_norm, normed_second, inverse_second = layer_norm(resid, ln2_gain, ln2_bias)
    mlp_in = both_halves(mlp_norm.astype(bf16))
    grad_mlp = (keep * grad_rows.astype(f32)).astype(bf16)
    grad_act = lax.optimization_barrier(contract(grad_mlp, w_down, 1, 1))
    up_proj = dot(mlp_in, w_up)
    activated, gelu_pull = jax.vjp(partial(jax.nn.gelu, approximate=True), up_proj)
    act_low = activated.astype(bf16)
    grad_up = gelu_pull(grad_act)[0].astype(bf16)
    pair = pair_sum(contract(grad_up[half:], w_up, 1, 1), contract(grad_up[:half], w_up, 1, 1))
    w_down_grad = contract(act_low, grad_mlp, 0, 0).astype(bf16)
    w_up_grad = contract(mlp_in, grad_up, 0, 0).astype(bf16)
    arrived, act_low, w_up_grad, w_down_grad = lax.optimization_barrier(
        (other_chip(pair), act_low, w_up_grad, w_down_grad)
    )
    early = lax.psum((w_up_grad, w_down_grad), "dp")
    grad_mlp_in = pair.astype(f32) + arrived.astype(f32)
    mlp_pair = pair_sum(dot(act_low[half:], w_down), dot(act_low[:half], w_down))
    mlp_arrived = other_chip(mlp_pair)
    grad_second, ln2_gain_grad, ln2_bias_grad = norm_back(
        grad_mlp_in, normed_second, inverse_second, ln2_gain
    )
    grad_resid = grad_own + grad_second
    grad_attn = both_halves((keep * grad_resid).astype(bf16))
    grad_heads = contract(w_out, grad_attn, 1, 1).astype(bf16)
    (g_cols,) = exchange(3, heads, (grad_heads, 0, 1))
    w_out_grad = dot(attn_cols, grad_attn).astype(bf16)

    pairs_far, carry = sweep_backward(
        far_views, q_cols, g_cols, heads_out, kv_far, log_norm, None
    )
    resid, mlp_pair, mlp_arrived, pairs_far = lax.optimization_barrier(
        (resid, mlp_pair, mlp_arrived, pairs_far)
    )
    mixed_own = (
        resid + keep * (mlp_pair.astype(f32) + mlp_arrived.astype(f32))
    ).astype(bf16)
    arrived = across(pairs_far)
    pairs_own, dq_cols = sweep_backward(
        own_views, q_cols, g_cols, heads_out, kv_own, log_norm, carry
    )
    pairs = (pairs_own.astype(f32) + arrived.astype(f32)).astype(bf16)
    grad_query, grad_pairs = exchange(4, heads, (dq_cols, 1, 0), (pairs, 0, 1))

    def partial_in(start):
        return contract(grad_query[:, start : start + half], w_query, 0, 1) + contract(
            grad_pairs[start : start + half], w_pairs, 1, 1
        )

    far_part, own_part = partial_in(half), partial_in(0)
    small = jnp.stack(
        [
            jnp.sum(far_part * normed_first[half:], axis=0)
            + jnp.sum(own_part * normed_first[:half], axis=0),
            jnp.sum(far_part, axis=0) + jnp.sum(own_part, axis=0),
            ln2_gain_grad * 0.5,
            ln2_bias_grad * 0.5,
        ]
        + [jnp.zeros((width,), f32)] * 4
    )
    late = (
        w_out_grad,
        contract(attn_in, grad_pairs, 0, 0).astype(bf16),
        contract(attn_in, grad_query, 0, 1).astype(bf16),
    )
    w_out_grad, w_pairs_grad, w_query_grad, grad_attn_in, small = last_sums(
        5, heads, late, far_part.astype(bf16), own_part, small
    )
    if devices > group:
        same = [list(range(at, devices, group)) for at in range(group)]
        w_out_grad, w_pairs_grad, w_query_grad, small = [
            lax.psum(array, "dp", axis_index_groups=same)
            for array in (w_out_grad, w_pairs_grad, w_query_grad, small)
        ]
    grad_first, _, _ = norm_back(
        grad_attn_in, normed_first[:half], inverse_first[:half], ln1_gain
    )
    tokens_grad_own = (grad_resid + grad_first).astype(bf16)
    w_pairs_grad = w_pairs_grad.astype(f32).reshape(width, heads, 2 * HEAD_DIM)

    def in_order(own):
        far = other_core(own)
        return jnp.where(
            core == 0, jnp.concatenate([own, far], axis=0), jnp.concatenate([far, own], axis=0)
        )

    return (
        in_order(mixed_own),
        in_order(tokens_grad_own),
        small[0],
        small[1],
        w_query_grad.astype(f32),
        w_pairs_grad[:, :, :HEAD_DIM].reshape(width, inner),
        w_pairs_grad[:, :, HEAD_DIM:].reshape(width, inner),
        w_out_grad.astype(f32),
        small[2],
        small[3],
        early[0].astype(f32),
        early[1].astype(f32),
    )


def solution(mesh):
    placed = (
        P("dp", None),
        P(),
        P(),
        P(),
        P(None, "tensor"),
        P(None, "tensor"),
        P(None, "tensor"),
        P("tensor", None),
        P(),
        P(),
        P(None, "tensor"),
        P("tensor", None),
        P("dp", None),
    )
    return jax.shard_map(
        shards,
        mesh=mesh,
        in_specs=placed,
        out_specs=(
            P("dp", None),
            P("dp", None),
            P(),
            P(),
            P(None, "tensor"),
            P(None, "tensor"),
            P(None, "tensor"),
            P("tensor", None),
            P(),
            P(),
            P(None, "tensor"),
            P("tensor", None),
        ),
        check_vma=False,
    )
```

```python
from functools import partial
import math

import jax
import jax.numpy as jnp
from jax import lax
from jax.experimental import pallas as pl
from jax.experimental.pallas import tpu as pltpu
from jax.sharding import PartitionSpec as P

HEAD_DIM = 64
VIEW_TOK = 1024
MAX_VIEWS = 8
LOG2E = math.log2(math.e)
VMEM_BYTES = 48 << 20
LOT = 128 << 10

norm_eps = 1e-05

bf16 = jnp.bfloat16
f32 = jnp.float32
dot = partial(jnp.dot, preferred_element_type=f32)


def contract(left, right, left_dim, right_dim):
    return lax.dot_general(
        left, right, (((left_dim,), (right_dim,)), ((), ())), preferred_element_type=f32
    )


def layer_norm(values, gain, shift):
    row_mean = jnp.mean(values, axis=-1, keepdims=True)
    centered = values - row_mean
    inverse = lax.rsqrt(jnp.mean(centered * centered, axis=-1, keepdims=True) + norm_eps)
    normed = centered * inverse
    return (normed * gain + shift, normed, inverse)


def norm_back(grad_norm, normed, inverse, gain):
    scaled = grad_norm * gain
    grad_input = inverse * (
        scaled
        - jnp.mean(scaled, axis=-1, keepdims=True)
        - normed * jnp.mean(scaled * normed, axis=-1, keepdims=True)
    )
    return (grad_input, jnp.sum(grad_norm * normed, axis=0), jnp.sum(grad_norm, axis=0))


def first_norm(core, tokens, gain, shift):
    row_count, width = tokens.shape
    block = row_count // 4

    def kernel(core_ref, tokens_ref, gain_ref, shift_ref, out_ref, normed_ref, inverse_ref):
        values, normed, inverse = layer_norm(
            tokens_ref[...].astype(f32), gain_ref[...], shift_ref[...]
        )
        out_ref[...] = values.astype(bf16)
        normed_ref[...] = normed
        inverse_ref[...] = inverse

    by_rows = pl.BlockSpec((block, width), lambda i, core_ref: (i, 0))
    row = pl.BlockSpec((1, width), lambda i, core_ref: (0, 0))
    return pl.pallas_call(
        kernel,
        grid_spec=pltpu.PrefetchScalarGridSpec(
            num_scalar_prefetch=1,
            grid=(4,),
            in_specs=[
                pl.BlockSpec((block, width), lambda i, core_ref: ((i + 2 * core_ref[0]) % 4, 0)),
                row,
                row,
            ],
            out_specs=[by_rows, by_rows, pl.BlockSpec((block, 1), lambda i, core_ref: (i, 0))],
        ),
        out_shape=[
            jax.ShapeDtypeStruct((row_count, width), bf16),
            jax.ShapeDtypeStruct((row_count, width), f32),
            jax.ShapeDtypeStruct((row_count, 1), f32),
        ],
        cost_estimate=pl.CostEstimate(
            flops=10 * row_count * width, bytes_accessed=8 * row_count * width, transcendentals=0
        ),
    )(core.reshape(1).astype(jnp.int32), tokens, gain.reshape(1, width), shift.reshape(1, width))


def sweep_forward(live_views, q_cols, kv, carry, last):
    count = q_cols.shape[1]
    keys = kv.shape[0]
    sum_rows = HEAD_DIM + 16
    bq, bk = 2048, 512

    def kernel(*refs):
        live_ref, q_ref, kv_ref = refs[:3]
        columns_ref = refs[-1]
        refs = refs[3:-1]
        if carry is not None:
            start = (refs[0][...], refs[1][...])
            refs = refs[2:]
        else:
            start = (jnp.full((1, bq), -1e30, f32), jnp.zeros((sum_rows, bq), f32))
        queries = jnp.concatenate([q_ref[...], jnp.zeros((HEAD_DIM, bq), bf16)], axis=0)

        @pl.when(pl.program_id(0) == 0)
        def _():
            columns_ref[HEAD_DIM:, :] = jnp.ones((16, keys), bf16)
            columns_ref[:HEAD_DIM, :] = kv_ref[...].T[HEAD_DIM:]

        def view_step(view, running):
            top, accum = running
            for part in range(VIEW_TOK // bk):
                first = pl.multiple_of(view * VIEW_TOK + part * bk, bk)
                scores = dot(kv_ref[pl.ds(first, bk), :], queries)
                new_top = jnp.maximum(top, jnp.max(scores, axis=0, keepdims=True))
                weights = jnp.exp2(scores - new_top).astype(bf16)
                accum = accum * jnp.exp2(top - new_top) + dot(
                    columns_ref[:, pl.ds(first, bk)], weights
                )
                top = new_top
            return (top, accum)

        top, accum = lax.fori_loop(0, live_ref[0], view_step, start)
        if last:
            total = accum[HEAD_DIM : HEAD_DIM + 1]
            heads_out = accum[:HEAD_DIM] / total
            refs[0][...] = heads_out
            refs[1][...] = heads_out.astype(bf16)
            refs[2][...] = top + jnp.log2(total)
        else:
            refs[0][...] = top
            refs[1][...] = accum

    def columns(rows):
        return pl.BlockSpec((rows, bq), lambda i: (0, i))

    in_specs = [
        pl.BlockSpec(memory_space=pltpu.SMEM),
        columns(HEAD_DIM),
        pl.BlockSpec(kv.shape, lambda i: (0, 0)),
    ]
    operands = [live_views, q_cols, kv]
    if carry is not None:
        in_specs += [columns(1), columns(sum_rows)]
        operands += list(carry)
    if last:
        shapes = [((HEAD_DIM, count), f32), ((HEAD_DIM, count), bf16), ((1, count), f32)]
    else:
        shapes = [((1, count), f32), ((sum_rows, count), f32)]
    return pl.pallas_call(
        kernel,
        grid=(count // bq,),
        in_specs=in_specs,
        out_specs=[columns(shape[0]) for shape, _ in shapes],
        out_shape=[jax.ShapeDtypeStruct(shape, kind) for shape, kind in shapes],
        scratch_shapes=[pltpu.VMEM((sum_rows, keys), bf16)],
        compiler_params=pltpu.CompilerParams(vmem_limit_bytes=VMEM_BYTES),
        cost_estimate=pl.CostEstimate(
            flops=16 * HEAD_DIM * count * keys, bytes_accessed=8 << 20, transcendentals=count * keys
        ),
    )(*operands)


def sweep_backward(live_views, q_cols, g_cols, heads_out, kv, log_norm, carry):
    count = q_cols.shape[1]
    keys = kv.shape[0]
    bq, bk = 1024, 512
    last = carry is not None

    def kernel(*refs):
        live_ref, q_ref, g_ref, heads_ref, kv_ref, norm_ref = refs[:6]
        carry_ref = refs[6] if last else None
        pairs_ref, out_ref, total_ref, rows_ref, delta_ref = refs[-5:]
        step = pl.program_id(0)

        @pl.when(step == 0)
        def _():
            total_ref[...] = carry_ref[...] if last else jnp.zeros_like(total_ref)
            rows_ref[...] = jnp.concatenate([q_ref[...], g_ref[...]], axis=0).T
            delta_ref[...] = jnp.sum(
                g_ref[...].astype(f32) * heads_ref[...], axis=0, keepdims=True
            )

        live = step * bk < live_ref[0] * VIEW_TOK

        @pl.when(live)
        def _():
            key_values = kv_ref[...]
            key_columns = key_values.T[:HEAD_DIM]
            empty = jnp.zeros((HEAD_DIM, bq), bf16)
            is_key = lax.broadcasted_iota(jnp.int32, (bq, 2 * HEAD_DIM), 1) < HEAD_DIM

            def parts(pair, accum):
                for bit in range(2):
                    span = pl.ds(pl.multiple_of((pair * 2 + bit) * bq, bq), bq)
                    scores = dot(key_values, jnp.concatenate([q_ref[:, span], empty], axis=0))
                    weights = jnp.exp2(scores - norm_ref[:, span])
                    grad_weights = dot(
                        key_values, jnp.concatenate([empty, g_ref[:, span]], axis=0)
                    )
                    grad_scores = (weights * (grad_weights - delta_ref[:, span])).astype(bf16)
                    rows = rows_ref[span, :]
                    none = jnp.zeros_like(rows)
                    accum += dot(weights.astype(bf16), jnp.where(is_key, none, rows))
                    accum += dot(grad_scores, jnp.where(is_key, rows, none))
                    total_ref[:, span] += dot(key_columns, grad_scores)
                return accum

            accum = lax.fori_loop(
                0, count // (2 * bq), parts, jnp.zeros((bk, 2 * HEAD_DIM), f32)
            )
            lane = lax.broadcasted_iota(jnp.int32, accum.shape, 1)
            pairs_ref[...] = jnp.where(lane < HEAD_DIM, accum * (1.0 / LOG2E), accum).astype(bf16)

        @pl.when(jnp.logical_not(live))
        def _():
            pairs_ref[...] = jnp.zeros_like(pairs_ref)

        @pl.when(step == pl.num_programs(0) - 1)
        def _():
            if last:
                out_ref[...] = (total_ref[...] * HEAD_DIM ** (-0.5)).astype(bf16)
            else:
                out_ref[...] = total_ref[...]

    def whole(array):
        return pl.BlockSpec(array.shape, lambda i: (0, 0))

    by_keys = pl.BlockSpec((bk, 2 * HEAD_DIM), lambda i: (i, 0))
    in_specs = [
        pl.BlockSpec(memory_space=pltpu.SMEM),
        whole(q_cols),
        whole(g_cols),
        whole(heads_out),
        by_keys,
        whole(log_norm),
    ]
    operands = [live_views, q_cols, g_cols, heads_out, kv, log_norm]
    if last:
        in_specs.append(whole(carry))
        operands.append(carry)
    return pl.pallas_call(
        kernel,
        grid=(keys // bk,),
        in_specs=in_specs,
        out_specs=[by_keys, pl.BlockSpec((HEAD_DIM, count), lambda i: (0, 0))],
        out_shape=[
            jax.ShapeDtypeStruct((keys, 2 * HEAD_DIM), bf16),
            jax.ShapeDtypeStruct((HEAD_DIM, count), bf16 if last else f32),
        ],
        scratch_shapes=[
            pltpu.VMEM((HEAD_DIM, count), f32),
            pltpu.VMEM((count, 2 * HEAD_DIM), bf16),
            pltpu.VMEM((1, count), f32),
        ],
        compiler_params=pltpu.CompilerParams(vmem_limit_bytes=VMEM_BYTES),
        cost_estimate=pl.CostEstimate(
            flops=40 * HEAD_DIM * count * keys, bytes_accessed=10 << 20, transcendentals=count * keys
        ),
    )(*operands)


MESH = pl.DeviceIdType.MESH


def greet(peers):
    barrier = pltpu.get_barrier_semaphore()
    for peer in peers:
        pl.semaphore_signal(barrier, inc=1, device_id=peer, device_id_type=MESH)
    pl.semaphore_wait(barrier, len(peers))


def window(start, size, axis):
    span = pl.ds(pl.multiple_of(start, size), size)
    return (span, slice(None)) if axis == 0 else (slice(None), span)


def exchange(number, ways, *items):
    def kernel(*refs):
        count = len(items)
        sources, targets = refs[:count], refs[count : 2 * count]
        own_sems, send_sems, recv_sems = refs[2 * count :]
        position = lax.axis_index("dp")
        place = position % (2 * ways) // 2
        base = position - 2 * place
        places = [lax.rem(place + distance, ways) for distance in range(ways)]
        greet([{"dp": base + 2 * places[distance]} for distance in range(1, ways)])
        copies = []
        for distance in range(1, ways):
            for index, (array, split, concat) in enumerate(items):
                size = array.shape[split] // ways
                copy = pltpu.make_async_remote_copy(
                    src_ref=sources[index].at[window(places[distance] * size, size, split)],
                    dst_ref=targets[index].at[
                        window(place * array.shape[concat], array.shape[concat], concat)
                    ],
                    send_sem=send_sems.at[index, distance],
                    recv_sem=recv_sems.at[index, distance],
                    device_id={"dp": base + 2 * places[distance]},
                    device_id_type=MESH,
                )
                copy.start()
                copies.append(copy)
        for index, (array, split, concat) in enumerate(items):
            size = array.shape[split] // ways
            copy = pltpu.make_async_copy(
                sources[index].at[window(place * size, size, split)],
                targets[index].at[
                    window(place * array.shape[concat], array.shape[concat], concat)
                ],
                own_sems.at[index],
            )
            copy.start()
            copies.append(copy)
        for copy in copies:
            copy.wait()

    def shape(array, split, concat):
        sizes = list(array.shape)
        sizes[split] //= ways
        sizes[concat] *= ways
        return jax.ShapeDtypeStruct(tuple(sizes), array.dtype)

    count = len(items)
    vmem = pl.BlockSpec(memory_space=pltpu.VMEM)
    moved = sum(array.size * array.dtype.itemsize for array, _, _ in items)
    return pl.pallas_call(
        kernel,
        in_specs=[vmem] * count,
        out_specs=[vmem] * count,
        out_shape=[shape(*item) for item in items],
        scratch_shapes=[
            pltpu.SemaphoreType.DMA((count,)),
            pltpu.SemaphoreType.DMA((count, ways)),
            pltpu.SemaphoreType.DMA((count, ways)),
        ],
        compiler_params=pltpu.CompilerParams(
            collective_id=number, has_side_effects=True, vmem_limit_bytes=16 << 20
        ),
        cost_estimate=pl.CostEstimate(flops=0, bytes_accessed=40 * moved, transcendentals=0),
    )(*[array for array, _, _ in items])


def last_sums(number, ways, grads, far_part, own_part, small, normed, inverse, gain, resid, mixed):
    chunks = []
    for index, grad in enumerate(grads):
        rows = grad.shape[0] * LOT // grad.size
        chunks += [(index, first, rows) for first in range(0, grad.shape[0], rows)]
    lots = len(chunks)
    rounds = 5

    def kernel(*refs):
        count = len(grads)
        sources = refs[:count]
        far_ref, own_ref, small_ref, normed_ref, inverse_ref, gain_ref, resid_ref, mixed_ref = refs[
            count : count + 8
        ]
        refs = refs[count + 8 :]
        results = refs[:count]
        tokens_ref, mixed_out_ref, small_sum_ref = refs[count : count + 3]
        refs = refs[count + 3 :]
        x_in, x_sums, z_in = refs[:lots], refs[lots : 2 * lots], refs[2 * lots : 3 * lots]
        core_in, pair_ref, chip_in, small_in, small_out = refs[3 * lots : 3 * lots + 5]
        sems = refs[3 * lots + 5 :]
        position = lax.axis_index("dp")
        slot = lax.axis_index("tensor")
        place = position % (2 * ways) // 2
        side = position % 2
        base = position - 2 * place
        across = {"dp": position + 1 - 2 * side}
        places = [lax.rem(place + distance, ways) for distance in range(ways)]
        peers = [{"dp": base + 2 * at} for at in places]
        partner = slot + 1 - 2 * lax.rem(slot, 2)
        chip = lax.rem(slot + 2, 4)
        core_to, chip_to = {"tensor": partner}, {"tensor": chip}
        even = place + 1 - 2 * lax.rem(place, 2)
        steps = [
            core_to,
            chip_to,
            across,
            {"dp": base + 2 * even},
            {"dp": base + 2 * lax.rem(place + 2, ways)},
        ]
        greet([across, core_to, chip_to] + peers[1:])
        pending = []

        def send(source, target, pair, at, to):
            copy = pltpu.make_async_remote_copy(
                src_ref=source,
                dst_ref=target,
                send_sem=sems[2 * pair].at[at],
                recv_sem=sems[2 * pair + 1].at[at],
                device_id=to,
                device_id_type=MESH,
            )
            copy.start()
            pending.append(copy)
            return copy

        mine_first = lax.rem(slot, 2) * own_ref.shape[0]
        own_rows = window(mine_first, own_ref.shape[0], 0)
        small_copy = send(small_ref, small_in.at[0], 1, 0, steps[0])
        core_copy = send(far_ref, core_in, 0, 0, core_to)
        across_copies = []

        def start_across(lot):
            index, first, rows = chunks[lot]
            half = rows // 2
            given = window(first + (1 - side) * half, half, 0)
            across_copies.append(send(sources[index].at[given], x_in[lot], 2, lot, across))

        for lot in range(3):
            start_across(lot)

        def small_round(at, copy):
            copy.wait_recv()
            total = (small_ref if at == 0 else small_out.at[at - 1])[...] + small_in[at]
            if at == rounds - 1:
                small_sum_ref[...] = total
                return None
            small_out[at] = total
            return send(small_out.at[at], small_in.at[at + 1], 1, at + 1, steps[at + 1])

        def reduce_across(lot):
            index, first, rows = chunks[lot]
            half, part = rows // 2, rows // 2 // ways
            across_copies[lot].wait_recv()
            kept = sources[index][window(first + side * half, half, 0)]
            x_sums[lot][...] = (kept.astype(f32) + x_in[lot][...].astype(f32)).astype(bf16)
            return [
                send(
                    x_sums[lot].at[window(places[distance] * part, part, 0)],
                    z_in[lot].at[distance - 1],
                    3,
                    lot * ways + distance,
                    peers[distance],
                )
                for distance in range(1, ways)
            ]

        def reduce_places(lot, copies):
            index, first, rows = chunks[lot]
            half, part = rows // 2, rows // 2 // ways
            total = x_sums[lot][window(place * part, part, 0)].astype(f32)
            for distance in range(1, ways):
                copies[distance - 1].wait_recv()
                total += z_in[lot][distance - 1].astype(f32)
            mine = window(first + side * half + place * part, part, 0)
            results[index][mine] = total.astype(bf16)
            return [
                send(
                    results[index].at[mine],
                    results[index].at[mine],
                    4,
                    lot * ways + distance,
                    peers[distance],
                )
                for distance in range(1, ways)
            ]

        def give_across(lot, copies):
            index, first, rows = chunks[lot]
            half = rows // 2
            for copy in copies:
                copy.wait_recv()
            mine = window(first + side * half, half, 0)
            return send(results[index].at[mine], results[index].at[mine], 5, lot, across)

        small_copy = small_round(0, small_copy)
        core_copy.wait_recv()
        pair_ref[...] = (own_ref[...] + core_in[...].astype(f32)).astype(bf16)
        chip_copy = send(pair_ref, chip_in, 6, 0, chip_to)
        mixed_copy = send(mixed_ref, mixed_out_ref.at[own_rows], 7, 0, core_to)
        mixed_own = pltpu.make_async_copy(mixed_ref, mixed_out_ref.at[own_rows], sems[-1].at[0])
        mixed_own.start()
        small_copy = small_round(1, small_copy)
        reduced, gathered, given = {}, {}, {}
        for step in range(lots + 4):
            if step + 3 < lots:
                start_across(step + 3)
            if step < lots:
                reduced[step] = reduce_across(step)
            if 2 <= step < lots + 2:
                gathered[step - 2] = reduce_places(step - 2, reduced[step - 2])
            if step >= 4:
                given[step - 4] = give_across(step - 4, gathered[step - 4])
            if step in (5, 9):
                small_copy = small_round(2 if step == 5 else 3, small_copy)
        chip_copy.wait_recv()
        strip = 64

        def norm_rows(at, none):
            first = pl.multiple_of(at * strip, strip)
            rows = pl.ds(first, strip)
            grad_norm = pair_ref[rows, :].astype(f32) + chip_in[rows, :].astype(f32)
            scaled = grad_norm * gain_ref[...]
            normed_rows = normed_ref[rows, :]
            grad_input = inverse_ref[rows, :] * (
                scaled
                - jnp.mean(scaled, axis=-1, keepdims=True)
                - normed_rows * jnp.mean(scaled * normed_rows, axis=-1, keepdims=True)
            )
            tokens_ref[pl.ds(pl.multiple_of(mine_first + first, strip), strip), :] = (
                resid_ref[rows, :] + grad_input
            ).astype(bf16)
            return none

        lax.fori_loop(0, own_ref.shape[0] // strip, norm_rows, 0)
        tokens_copy = send(tokens_ref.at[own_rows], tokens_ref.at[own_rows], 8, 0, core_to)
        small_round(4, small_copy)
        mixed_own.wait()
        mixed_copy.wait_recv()
        tokens_copy.wait_recv()
        for lot in range(lots):
            given[lot].wait_recv()
        for copy in pending:
            copy.wait_send()

    vmem = pl.BlockSpec(memory_space=pltpu.VMEM)
    shapes = [jax.ShapeDtypeStruct(grad.shape, bf16) for grad in grads]
    both = jax.ShapeDtypeStruct((2 * own_part.shape[0], own_part.shape[1]), bf16)
    shapes += [both, both, jax.ShapeDtypeStruct(small.shape, f32)]
    wide = [grads[index].shape[1] for index, _, _ in chunks]
    scratch = [pltpu.VMEM((lot[2] // 2, w), bf16) for lot, w in zip(chunks, wide)]
    scratch += [pltpu.VMEM((lot[2] // 2, w), bf16) for lot, w in zip(chunks, wide)]
    scratch += [pltpu.VMEM((ways - 1, lot[2] // 2 // ways, w), bf16) for lot, w in zip(chunks, wide)]
    scratch += [pltpu.VMEM(far_part.shape, bf16)] * 3
    scratch += [pltpu.VMEM((rounds,) + small.shape, f32)] * 2
    for number_of in (1, rounds, lots, lots * ways, lots * ways, lots, 1, 1, 1):
        scratch += [pltpu.SemaphoreType.DMA((number_of,))] * 2
    scratch.append(pltpu.SemaphoreType.DMA((1,)))
    return pl.pallas_call(
        kernel,
        in_specs=[vmem] * (len(grads) + 8),
        out_specs=[vmem] * len(shapes),
        out_shape=shapes,
        scratch_shapes=scratch,
        compiler_params=pltpu.CompilerParams(
            collective_id=number, has_side_effects=True, vmem_limit_bytes=44 << 20
        ),
        cost_estimate=pl.CostEstimate(flops=0, bytes_accessed=150 << 20, transcendentals=0),
    )(*grads, far_part, own_part, small, normed, inverse, gain, resid, mixed)


def shards(
    tokens,
    views,
    ln1_gain,
    ln1_bias,
    w_query,
    w_key,
    w_value,
    w_out,
    ln2_gain,
    ln2_bias,
    w_up,
    w_down,
    cotangent,
):
    row_count, width = tokens.shape
    inner = w_query.shape[1]
    heads = inner // HEAD_DIM
    half = row_count // 2
    group = MAX_VIEWS * VIEW_TOK // row_count
    devices = lax.axis_size("dp")
    assert row_count == VIEW_TOK and group == 2 * heads and lax.axis_size("tensor") == 4
    position = lax.axis_index("dp")
    block = position % group
    side = block % 2
    core = lax.axis_index("tensor") % 2
    scene_views = lax.dynamic_index_in_dim(views, position // group, keepdims=False)
    own_views = ((scene_views + 1 - side) // 2).reshape(1)
    far_views = ((scene_views + side) // 2).reshape(1)
    keep = (block < scene_views).astype(f32)
    def across(block):
        return lax.ppermute(block, "dp", [(i, i ^ 1) for i in range(devices)])

    def other_core(block):
        return lax.ppermute(block, "tensor", [(i, i ^ 1) for i in range(4)])

    def other_chip(block):
        return lax.ppermute(block, "tensor", [(i, i ^ 2) for i in range(4)])

    def own_first(block):
        return jnp.where(core == 0, block, jnp.concatenate([block[half:], block[:half]], axis=0))

    def pair_sum(far_part, own_part):
        arrived = other_core(far_part.astype(bf16))
        return (own_part + arrived.astype(f32)).astype(bf16)

    def both_halves(own):
        return jnp.concatenate([own, other_core(own)], axis=0)

    grad_rows = own_first(cotangent)
    inputs_own = jnp.where(core == 0, tokens[:half], tokens[half:]).astype(f32)
    grad_own = grad_rows[:half].astype(f32)

    attn_in, normed_first, inverse_first = first_norm(core, tokens, ln1_gain, ln1_bias)
    w_pairs = jnp.concatenate(
        [w_key.reshape(width, heads, HEAD_DIM), w_value.reshape(width, heads, HEAD_DIM)], axis=2
    ).reshape(width, 2 * inner)
    kv_low = dot(attn_in, w_pairs).astype(bf16)
    query_low = (contract(w_query, attn_in, 0, 1) * (LOG2E * HEAD_DIM ** (-0.5))).astype(bf16)
    q_cols, kv_own = exchange(1, heads, (query_low, 0, 1), (kv_low, 1, 0))
    kv_far = across(kv_own)

    carry = sweep_forward(own_views, q_cols, kv_own, None, False)
    heads_out, heads_low, log_norm = sweep_forward(far_views, q_cols, kv_far, carry, True)
    (attn_cols,) = exchange(2, heads, (heads_low, 1, 0))

    pair = pair_sum(
        contract(attn_cols[:, half:], w_out, 0, 0), contract(attn_cols[:, :half], w_out, 0, 0)
    )
    resid = inputs_own + keep * (pair.astype(f32) + other_chip(pair).astype(f32))
    mlp_norm, normed_second, inverse_second = layer_norm(resid, ln2_gain, ln2_bias)
    mlp_in = both_halves(mlp_norm.astype(bf16))
    grad_mlp = (keep * grad_rows.astype(f32)).astype(bf16)
    grad_act = lax.optimization_barrier(contract(grad_mlp, w_down, 1, 1))
    up_proj = dot(mlp_in, w_up)
    activated, gelu_pull = jax.vjp(partial(jax.nn.gelu, approximate=True), up_proj)
    act_low = activated.astype(bf16)
    grad_up = gelu_pull(grad_act)[0].astype(bf16)
    pair = pair_sum(contract(grad_up[half:], w_up, 1, 1), contract(grad_up[:half], w_up, 1, 1))
    w_down_grad = contract(act_low, grad_mlp, 0, 0).astype(bf16)
    w_up_grad = contract(mlp_in, grad_up, 0, 0).astype(bf16)
    arrived, act_low, w_up_grad, w_down_grad = lax.optimization_barrier(
        (other_chip(pair), act_low, w_up_grad, w_down_grad)
    )
    early = lax.psum((w_up_grad, w_down_grad), "dp")
    grad_mlp_in = pair.astype(f32) + arrived.astype(f32)
    mlp_pair = pair_sum(dot(act_low[half:], w_down), dot(act_low[:half], w_down))
    mlp_arrived = other_chip(mlp_pair)
    grad_second, ln2_gain_grad, ln2_bias_grad = norm_back(
        grad_mlp_in, normed_second, inverse_second, ln2_gain
    )
    grad_resid = grad_own + grad_second
    grad_attn = both_halves((keep * grad_resid).astype(bf16))
    grad_heads = contract(w_out, grad_attn, 1, 1).astype(bf16)
    (g_cols,) = exchange(3, heads, (grad_heads, 0, 1))
    w_out_grad = dot(attn_cols, grad_attn).astype(bf16)

    pairs_far, carry = sweep_backward(
        far_views, q_cols, g_cols, heads_out, kv_far, log_norm, None
    )
    resid, mlp_pair, mlp_arrived, pairs_far = lax.optimization_barrier(
        (resid, mlp_pair, mlp_arrived, pairs_far)
    )
    mixed_own = (
        resid + keep * (mlp_pair.astype(f32) + mlp_arrived.astype(f32))
    ).astype(bf16)
    arrived = across(pairs_far)
    pairs_own, dq_cols = sweep_backward(
        own_views, q_cols, g_cols, heads_out, kv_own, log_norm, carry
    )
    pairs = (pairs_own.astype(f32) + arrived.astype(f32)).astype(bf16)
    grad_query, grad_pairs = exchange(4, heads, (dq_cols, 1, 0), (pairs, 0, 1))

    def partial_in(start):
        return contract(grad_query[:, start : start + half], w_query, 0, 1) + contract(
            grad_pairs[start : start + half], w_pairs, 1, 1
        )

    far_part, own_part = partial_in(half), partial_in(0)
    small = jnp.stack(
        [
            jnp.sum(far_part * normed_first[half:], axis=0)
            + jnp.sum(own_part * normed_first[:half], axis=0),
            jnp.sum(far_part, axis=0) + jnp.sum(own_part, axis=0),
            ln2_gain_grad * 0.5,
            ln2_bias_grad * 0.5,
        ]
        + [jnp.zeros((width,), f32)] * 4
    )
    late = (
        w_out_grad,
        contract(attn_in, grad_pairs, 0, 0).astype(bf16),
        contract(attn_in, grad_query, 0, 1).astype(bf16),
    )
    w_out_grad, w_pairs_grad, w_query_grad, tokens_grad, mixed, small = last_sums(
        5,
        heads,
        late,
        far_part.astype(bf16),
        own_part,
        small,
        normed_first[:half],
        inverse_first[:half],
        ln1_gain.reshape(1, width),
        grad_resid,
        mixed_own,
    )
    if devices > group:
        same = [list(range(at, devices, group)) for at in range(group)]
        w_out_grad, w_pairs_grad, w_query_grad, small = [
            lax.psum(array, "dp", axis_index_groups=same)
            for array in (w_out_grad, w_pairs_grad, w_query_grad, small)
        ]
    w_pairs_grad = w_pairs_grad.astype(f32).reshape(width, heads, 2 * HEAD_DIM)

    return (
        mixed,
        tokens_grad,
        small[0],
        small[1],
        w_query_grad.astype(f32),
        w_pairs_grad[:, :, :HEAD_DIM].reshape(width, inner),
        w_pairs_grad[:, :, HEAD_DIM:].reshape(width, inner),
        w_out_grad.astype(f32),
        small[2],
        small[3],
        early[0].astype(f32),
        early[1].astype(f32),
    )


def solution(mesh):
    placed = (
        P("dp", None),
        P(),
        P(),
        P(),
        P(None, "tensor"),
        P(None, "tensor"),
        P(None, "tensor"),
        P("tensor", None),
        P(),
        P(),
        P(None, "tensor"),
        P("tensor", None),
        P("dp", None),
    )
    return jax.shard_map(
        shards,
        mesh=mesh,
        in_specs=placed,
        out_specs=(
            P("dp", None),
            P("dp", None),
            P(),
            P(),
            P(None, "tensor"),
            P(None, "tensor"),
            P(None, "tensor"),
            P("tensor", None),
            P(),
            P(),
            P(None, "tensor"),
            P("tensor", None),
        ),
        check_vma=False,
    )
```

```python
from functools import partial
import math

import jax
import jax.numpy as jnp
from jax import lax
from jax.experimental import pallas as pl
from jax.experimental.pallas import tpu as pltpu
from jax.sharding import PartitionSpec as P

HEAD_DIM = 64
VIEW_TOK = 1024
MAX_VIEWS = 8
LOG2E = math.log2(math.e)
VMEM_BYTES = 48 << 20
LOT = 128 << 10

norm_eps = 1e-05

bf16 = jnp.bfloat16
f32 = jnp.float32
dot = partial(jnp.dot, preferred_element_type=f32)


def contract(left, right, left_dim, right_dim):
    return lax.dot_general(
        left, right, (((left_dim,), (right_dim,)), ((), ())), preferred_element_type=f32
    )


def layer_norm(values, gain, shift):
    row_mean = jnp.mean(values, axis=-1, keepdims=True)
    centered = values - row_mean
    inverse = lax.rsqrt(jnp.mean(centered * centered, axis=-1, keepdims=True) + norm_eps)
    normed = centered * inverse
    return (normed * gain + shift, normed, inverse)


def norm_back(grad_norm, normed, inverse, gain):
    scaled = grad_norm * gain
    grad_input = inverse * (
        scaled
        - jnp.mean(scaled, axis=-1, keepdims=True)
        - normed * jnp.mean(scaled * normed, axis=-1, keepdims=True)
    )
    return (grad_input, jnp.sum(grad_norm * normed, axis=0), jnp.sum(grad_norm, axis=0))


def first_norm(core, tokens, gain, shift):
    row_count, width = tokens.shape
    block = row_count // 4

    def kernel(core_ref, tokens_ref, gain_ref, shift_ref, out_ref, normed_ref, inverse_ref):
        values, normed, inverse = layer_norm(
            tokens_ref[...].astype(f32), gain_ref[...], shift_ref[...]
        )
        out_ref[...] = values.astype(bf16)
        normed_ref[...] = normed
        inverse_ref[...] = inverse

    by_rows = pl.BlockSpec((block, width), lambda i, core_ref: (i, 0))
    row = pl.BlockSpec((1, width), lambda i, core_ref: (0, 0))
    return pl.pallas_call(
        kernel,
        grid_spec=pltpu.PrefetchScalarGridSpec(
            num_scalar_prefetch=1,
            grid=(4,),
            in_specs=[
                pl.BlockSpec((block, width), lambda i, core_ref: ((i + 2 * core_ref[0]) % 4, 0)),
                row,
                row,
            ],
            out_specs=[by_rows, by_rows, pl.BlockSpec((block, 1), lambda i, core_ref: (i, 0))],
        ),
        out_shape=[
            jax.ShapeDtypeStruct((row_count, width), bf16),
            jax.ShapeDtypeStruct((row_count, width), f32),
            jax.ShapeDtypeStruct((row_count, 1), f32),
        ],
        cost_estimate=pl.CostEstimate(
            flops=10 * row_count * width, bytes_accessed=8 * row_count * width, transcendentals=0
        ),
    )(core.reshape(1).astype(jnp.int32), tokens, gain.reshape(1, width), shift.reshape(1, width))


def sweep_forward(live_views, q_cols, kv, carry, last):
    count = q_cols.shape[1]
    keys = kv.shape[0]
    sum_rows = HEAD_DIM + 16
    bq, bk = 2048, 512

    def kernel(*refs):
        live_ref, q_ref, kv_ref = refs[:3]
        columns_ref = refs[-1]
        refs = refs[3:-1]
        if carry is not None:
            start = (refs[0][...], refs[1][...])
            refs = refs[2:]
        else:
            start = (jnp.full((1, bq), -1e30, f32), jnp.zeros((sum_rows, bq), f32))
        queries = jnp.concatenate([q_ref[...], jnp.zeros((HEAD_DIM, bq), bf16)], axis=0)

        @pl.when(pl.program_id(0) == 0)
        def _():
            columns_ref[HEAD_DIM:, :] = jnp.ones((16, keys), bf16)
            columns_ref[:HEAD_DIM, :] = kv_ref[...].T[HEAD_DIM:]

        def view_step(view, running):
            top, accum = running
            for part in range(VIEW_TOK // bk):
                first = pl.multiple_of(view * VIEW_TOK + part * bk, bk)
                scores = dot(kv_ref[pl.ds(first, bk), :], queries)
                new_top = jnp.maximum(top, jnp.max(scores, axis=0, keepdims=True))
                weights = jnp.exp2(scores - new_top).astype(bf16)
                accum = accum * jnp.exp2(top - new_top) + dot(
                    columns_ref[:, pl.ds(first, bk)], weights
                )
                top = new_top
            return (top, accum)

        top, accum = lax.fori_loop(0, live_ref[0], view_step, start)
        if last:
            total = accum[HEAD_DIM : HEAD_DIM + 1]
            heads_out = accum[:HEAD_DIM] / total
            refs[0][...] = heads_out
            refs[1][...] = heads_out.astype(bf16)
            refs[2][...] = top + jnp.log2(total)
        else:
            refs[0][...] = top
            refs[1][...] = accum

    def columns(rows):
        return pl.BlockSpec((rows, bq), lambda i: (0, i))

    in_specs = [
        pl.BlockSpec(memory_space=pltpu.SMEM),
        columns(HEAD_DIM),
        pl.BlockSpec(kv.shape, lambda i: (0, 0)),
    ]
    operands = [live_views, q_cols, kv]
    if carry is not None:
        in_specs += [columns(1), columns(sum_rows)]
        operands += list(carry)
    if last:
        shapes = [((HEAD_DIM, count), f32), ((HEAD_DIM, count), bf16), ((1, count), f32)]
    else:
        shapes = [((1, count), f32), ((sum_rows, count), f32)]
    return pl.pallas_call(
        kernel,
        grid=(count // bq,),
        in_specs=in_specs,
        out_specs=[columns(shape[0]) for shape, _ in shapes],
        out_shape=[jax.ShapeDtypeStruct(shape, kind) for shape, kind in shapes],
        scratch_shapes=[pltpu.VMEM((sum_rows, keys), bf16)],
        compiler_params=pltpu.CompilerParams(vmem_limit_bytes=VMEM_BYTES),
        cost_estimate=pl.CostEstimate(
            flops=16 * HEAD_DIM * count * keys, bytes_accessed=8 << 20, transcendentals=count * keys
        ),
    )(*operands)


MESH = pl.DeviceIdType.MESH


def greet(peers):
    barrier = pltpu.get_barrier_semaphore()
    for peer in peers:
        pl.semaphore_signal(barrier, inc=1, device_id=peer, device_id_type=MESH)
    pl.semaphore_wait(barrier, len(peers))


def window(start, size, axis):
    span = pl.ds(pl.multiple_of(start, size), size)
    return (span, slice(None)) if axis == 0 else (slice(None), span)


def exchange(number, ways, *items):
    def kernel(*refs):
        count = len(items)
        sources, targets = refs[:count], refs[count : 2 * count]
        own_sems, send_sems, recv_sems = refs[2 * count :]
        position = lax.axis_index("dp")
        place = position % (2 * ways) // 2
        base = position - 2 * place
        places = [lax.rem(place + distance, ways) for distance in range(ways)]
        greet([{"dp": base + 2 * places[distance]} for distance in range(1, ways)])
        copies = []
        for distance in range(1, ways):
            for index, (array, split, concat) in enumerate(items):
                size = array.shape[split] // ways
                copy = pltpu.make_async_remote_copy(
                    src_ref=sources[index].at[window(places[distance] * size, size, split)],
                    dst_ref=targets[index].at[
                        window(place * array.shape[concat], array.shape[concat], concat)
                    ],
                    send_sem=send_sems.at[index, distance],
                    recv_sem=recv_sems.at[index, distance],
                    device_id={"dp": base + 2 * places[distance]},
                    device_id_type=MESH,
                )
                copy.start()
                copies.append(copy)
        for index, (array, split, concat) in enumerate(items):
            size = array.shape[split] // ways
            copy = pltpu.make_async_copy(
                sources[index].at[window(place * size, size, split)],
                targets[index].at[
                    window(place * array.shape[concat], array.shape[concat], concat)
                ],
                own_sems.at[index],
            )
            copy.start()
            copies.append(copy)
        for copy in copies:
            copy.wait()

    def shape(array, split, concat):
        sizes = list(array.shape)
        sizes[split] //= ways
        sizes[concat] *= ways
        return jax.ShapeDtypeStruct(tuple(sizes), array.dtype)

    count = len(items)
    vmem = pl.BlockSpec(memory_space=pltpu.VMEM)
    moved = sum(array.size * array.dtype.itemsize for array, _, _ in items)
    return pl.pallas_call(
        kernel,
        in_specs=[vmem] * count,
        out_specs=[vmem] * count,
        out_shape=[shape(*item) for item in items],
        scratch_shapes=[
            pltpu.SemaphoreType.DMA((count,)),
            pltpu.SemaphoreType.DMA((count, ways)),
            pltpu.SemaphoreType.DMA((count, ways)),
        ],
        compiler_params=pltpu.CompilerParams(
            collective_id=number, has_side_effects=True, vmem_limit_bytes=16 << 20
        ),
        cost_estimate=pl.CostEstimate(flops=0, bytes_accessed=40 * moved, transcendentals=0),
    )(*[array for array, _, _ in items])


def sweep_backward(number, ways, bias, q_cols, g_cols, heads_out, kv_far, kv_own, log_norm, grads):
    count = q_cols.shape[1]
    keys = kv_own.shape[0]
    bq, bk = 1024, 512
    steps = 2 * keys // VIEW_TOK
    rows_of, width = grads[0].shape
    lot_rows = rows_of // steps
    half, part = lot_rows // 2, lot_rows // 2 // ways

    def kernel(*refs):
        masked = bias is not None
        bias_ref = refs[0] if masked else None
        refs = refs[1:] if masked else refs
        q_ref, g_ref, heads_ref, far_ref, own_ref, norm_ref = refs[:6]
        sources, pairs_ref, out_ref, results = refs[6:8], refs[8], refs[9], refs[10:12]
        total_ref, rows_ref, delta_ref, kv_ref, given_ref, met_ref, x_in, x_sums, z_in = refs[12:21]
        sems = refs[21:]
        position = lax.axis_index("dp")
        place = position % (2 * ways) // 2
        side = position % 2
        base = position - 2 * place
        across = {"dp": position + 1 - 2 * side}
        places = [lax.rem(place + distance, ways) for distance in range(ways)]
        peers = [{"dp": base + 2 * at} for at in places]
        greet([across] + peers[1:])

        def remote(source, target, kind, at, to):
            return pltpu.make_async_remote_copy(
                src_ref=source,
                dst_ref=target,
                send_sem=sems[2 * kind].at[at],
                recv_sem=sems[2 * kind + 1].at[at],
                device_id=to,
                device_id_type=MESH,
            )

        def over_x(which, lot):
            given = window(lot * lot_rows + (1 - side) * half, half, 0)
            slot = which * steps + lot
            return remote(sources[which].at[given], x_in.at[slot], 0, slot, across)

        def to_places(which, lot, distance):
            slot = which * steps + lot
            return remote(
                x_sums.at[slot, window(places[distance] * part, part, 0)[0]],
                z_in.at[slot, distance - 1],
                1,
                slot * ways + distance,
                peers[distance],
            )

        def from_place(which, lot, distance):
            slot = which * steps + lot
            mine = results[which].at[window(lot * lot_rows + side * half + place * part, part, 0)]
            return remote(mine, mine, 2, slot * ways + distance, peers[distance])

        def back_over_x(which, lot):
            mine = results[which].at[window(lot * lot_rows + side * half, half, 0)]
            return remote(mine, mine, 3, which * steps + lot, across)

        def far_pairs(view):
            span = window(view * VIEW_TOK, VIEW_TOK, 0)
            return remote(given_ref.at[span], met_ref.at[span], 4, view, across)

        def start_lot(lot):
            for which in range(2):
                over_x(which, lot).start()

        def reduce_across(lot):
            for which in range(2):
                slot = which * steps + lot
                over_x(which, lot).wait_recv()
                kept = sources[which][window(lot * lot_rows + side * half, half, 0)]
                x_sums[slot] = (kept.astype(f32) + x_in[slot].astype(f32)).astype(bf16)
                for distance in range(1, ways):
                    to_places(which, lot, distance).start()

        def reduce_places(lot):
            for which in range(2):
                slot = which * steps + lot
                total = x_sums[slot, window(place * part, part, 0)[0], :].astype(f32)
                for distance in range(1, ways):
                    to_places(which, lot, distance).wait_recv()
                    total += z_in[slot, distance - 1].astype(f32)
                mine = window(lot * lot_rows + side * half + place * part, part, 0)
                results[which][mine] = total.astype(bf16)
                for distance in range(1, ways):
                    from_place(which, lot, distance).start()

        def give_across(lot):
            for which in range(2):
                for distance in range(1, ways):
                    from_place(which, lot, distance).wait_recv()
                back_over_x(which, lot).start()

        start_lot(0)
        start_lot(1)
        total_ref[...] = jnp.zeros_like(total_ref)
        rows_ref[...] = jnp.concatenate([q_ref[...], g_ref[...]], axis=0).T
        delta_ref[...] = jnp.sum(g_ref[...].astype(f32) * heads_ref[...], axis=0, keepdims=True)
        kv_ref[:keys, :] = far_ref[...]
        kv_ref[keys:, :] = own_ref[...]

        def key_block(step, at):
            span_keys = pl.ds(pl.multiple_of(step * VIEW_TOK + at * bk, bk), bk)
            key_values = kv_ref[span_keys, :]
            key_columns = key_values.T[:HEAD_DIM]
            empty = jnp.zeros((HEAD_DIM, bq), bf16)
            is_key = lax.broadcasted_iota(jnp.int32, (bq, 2 * HEAD_DIM), 1) < HEAD_DIM

            def parts(pair, accum):
                for bit in range(2):
                    span = pl.ds(pl.multiple_of((pair * 2 + bit) * bq, bq), bq)
                    scores = dot(key_values, jnp.concatenate([q_ref[:, span], empty], axis=0))
                    if masked:
                        scores += bias_ref[step]
                    weights = jnp.exp2(scores - norm_ref[:, span])
                    grad_weights = dot(
                        key_values, jnp.concatenate([empty, g_ref[:, span]], axis=0)
                    )
                    grad_scores = (weights * (grad_weights - delta_ref[:, span])).astype(bf16)
                    rows = rows_ref[span, :]
                    none = jnp.zeros_like(rows)
                    accum += dot(weights.astype(bf16), jnp.where(is_key, none, rows))
                    accum += dot(grad_scores, jnp.where(is_key, rows, none))
                    total_ref[:, span] += dot(key_columns, grad_scores)
                return accum

            accum = lax.fori_loop(
                0, count // (2 * bq), parts, jnp.zeros((bk, 2 * HEAD_DIM), f32)
            )
            lane = lax.broadcasted_iota(jnp.int32, accum.shape, 1)
            accum = jnp.where(lane < HEAD_DIM, accum * (1.0 / LOG2E), accum)

            @pl.when(step < steps // 2)
            def _():
                given_ref[span_keys, :] = accum.astype(bf16)

            @pl.when(step >= steps // 2)
            def _():
                rows = pl.ds(pl.multiple_of(step * VIEW_TOK + at * bk - keys, bk), bk)
                pairs_ref[rows, :] = (accum + met_ref[rows, :].astype(f32)).astype(bf16)

        def view_step(step, none):
            @pl.when(step + 2 < steps)
            def _():
                start_lot(step + 2)

            reduce_across(step)

            @pl.when(step >= 1)
            def _():
                reduce_places(step - 1)

            @pl.when(step >= 2)
            def _():
                give_across(step - 2)

            @pl.when(step >= steps // 2)
            def _():
                far_pairs(step - steps // 2).wait_recv()

            def blocks(at, none):
                key_block(step, at)
                return none

            lax.fori_loop(0, VIEW_TOK // bk, blocks, 0)

            @pl.when(step < steps // 2)
            def _():
                far_pairs(step).start()

            return none

        lax.fori_loop(0, steps, view_step, 0)
        reduce_places(steps - 1)
        give_across(steps - 2)
        out_ref[...] = (total_ref[...] * HEAD_DIM ** (-0.5)).astype(bf16)
        give_across(steps - 1)

        def finish(lot, none):
            for which in range(2):
                over_x(which, lot).wait_send()
                back_over_x(which, lot).wait_recv()
                back_over_x(which, lot).wait_send()
                for distance in range(1, ways):
                    to_places(which, lot, distance).wait_send()
                    from_place(which, lot, distance).wait_send()

            return none

        lax.fori_loop(0, steps, finish, 0)
        for view in range(steps // 2):
            far_pairs(view).wait_send()

    vmem = pl.BlockSpec(memory_space=pltpu.VMEM)
    operands = [q_cols, g_cols, heads_out, kv_far, kv_own, log_norm] + list(grads)
    in_specs = [vmem] * len(operands)
    if bias is not None:
        operands = [bias] + operands
        in_specs = [pl.BlockSpec(memory_space=pltpu.SMEM)] + in_specs
    lots = 2 * steps
    scratch = [
        pltpu.VMEM((HEAD_DIM, count), f32),
        pltpu.VMEM((count, 2 * HEAD_DIM), bf16),
        pltpu.VMEM((1, count), f32),
        pltpu.VMEM((2 * keys, 2 * HEAD_DIM), bf16),
        pltpu.VMEM((keys, 2 * HEAD_DIM), bf16),
        pltpu.VMEM((keys, 2 * HEAD_DIM), bf16),
        pltpu.VMEM((lots, half, width), bf16),
        pltpu.VMEM((lots, half, width), bf16),
        pltpu.VMEM((lots, ways - 1, part, width), bf16),
    ]
    for number_of in (lots, lots * ways, lots * ways, lots, steps // 2):
        scratch += [pltpu.SemaphoreType.DMA((number_of,))] * 2
    return pl.pallas_call(
        kernel,
        in_specs=in_specs,
        out_specs=[vmem] * 4,
        out_shape=[
            jax.ShapeDtypeStruct((keys, 2 * HEAD_DIM), bf16),
            jax.ShapeDtypeStruct((HEAD_DIM, count), bf16),
        ]
        + [jax.ShapeDtypeStruct(grad.shape, bf16) for grad in grads],
        scratch_shapes=scratch,
        compiler_params=pltpu.CompilerParams(
            collective_id=number, has_side_effects=True, vmem_limit_bytes=VMEM_BYTES
        ),
        cost_estimate=pl.CostEstimate(
            flops=80 * HEAD_DIM * count * keys,
            bytes_accessed=20 << 20,
            transcendentals=2 * count * keys,
        ),
    )(*operands)


def last_sums(number, ways, grads, far_part, own_part, small, normed, inverse, gain, resid, mixed):
    chunks = []
    for index, grad in enumerate(grads):
        rows = grad.shape[0] * LOT // grad.size
        chunks += [(index, first, rows) for first in range(0, grad.shape[0], rows)]
    lots = len(chunks)
    rounds = 5

    def kernel(*refs):
        count = len(grads)
        sources = refs[:count]
        far_ref, own_ref, small_ref, normed_ref, inverse_ref, gain_ref, resid_ref, mixed_ref = refs[
            count : count + 8
        ]
        refs = refs[count + 8 :]
        results = refs[:count]
        tokens_ref, mixed_out_ref, small_sum_ref = refs[count : count + 3]
        refs = refs[count + 3 :]
        x_in, x_sums, z_in = refs[:lots], refs[lots : 2 * lots], refs[2 * lots : 3 * lots]
        core_in, pair_ref, chip_in, small_in, small_out = refs[3 * lots : 3 * lots + 5]
        sems = refs[3 * lots + 5 :]
        position = lax.axis_index("dp")
        slot = lax.axis_index("tensor")
        place = position % (2 * ways) // 2
        side = position % 2
        base = position - 2 * place
        across = {"dp": position + 1 - 2 * side}
        places = [lax.rem(place + distance, ways) for distance in range(ways)]
        peers = [{"dp": base + 2 * at} for at in places]
        partner = slot + 1 - 2 * lax.rem(slot, 2)
        chip = lax.rem(slot + 2, 4)
        core_to, chip_to = {"tensor": partner}, {"tensor": chip}
        even = place + 1 - 2 * lax.rem(place, 2)
        steps = [
            core_to,
            chip_to,
            across,
            {"dp": base + 2 * even},
            {"dp": base + 2 * lax.rem(place + 2, ways)},
        ]
        greet([across, core_to, chip_to] + peers[1:])
        pending = []

        def send(source, target, pair, at, to):
            copy = pltpu.make_async_remote_copy(
                src_ref=source,
                dst_ref=target,
                send_sem=sems[2 * pair].at[at],
                recv_sem=sems[2 * pair + 1].at[at],
                device_id=to,
                device_id_type=MESH,
            )
            copy.start()
            pending.append(copy)
            return copy

        mine_first = lax.rem(slot, 2) * own_ref.shape[0]
        own_rows = window(mine_first, own_ref.shape[0], 0)
        small_copy = send(small_ref, small_in.at[0], 1, 0, steps[0])
        core_copy = send(far_ref, core_in, 0, 0, core_to)
        across_copies = []

        def start_across(lot):
            index, first, rows = chunks[lot]
            half = rows // 2
            given = window(first + (1 - side) * half, half, 0)
            across_copies.append(send(sources[index].at[given], x_in[lot], 2, lot, across))

        for lot in range(3):
            start_across(lot)

        def small_round(at, copy):
            copy.wait_recv()
            total = (small_ref if at == 0 else small_out.at[at - 1])[...] + small_in[at]
            if at == rounds - 1:
                small_sum_ref[...] = total
                return None
            small_out[at] = total
            return send(small_out.at[at], small_in.at[at + 1], 1, at + 1, steps[at + 1])

        def reduce_across(lot):
            index, first, rows = chunks[lot]
            half, part = rows // 2, rows // 2 // ways
            across_copies[lot].wait_recv()
            kept = sources[index][window(first + side * half, half, 0)]
            x_sums[lot][...] = (kept.astype(f32) + x_in[lot][...].astype(f32)).astype(bf16)
            return [
                send(
                    x_sums[lot].at[window(places[distance] * part, part, 0)],
                    z_in[lot].at[distance - 1],
                    3,
                    lot * ways + distance,
                    peers[distance],
                )
                for distance in range(1, ways)
            ]

        def reduce_places(lot, copies):
            index, first, rows = chunks[lot]
            half, part = rows // 2, rows // 2 // ways
            total = x_sums[lot][window(place * part, part, 0)].astype(f32)
            for distance in range(1, ways):
                copies[distance - 1].wait_recv()
                total += z_in[lot][distance - 1].astype(f32)
            mine = window(first + side * half + place * part, part, 0)
            results[index][mine] = total.astype(bf16)
            return [
                send(
                    results[index].at[mine],
                    results[index].at[mine],
                    4,
                    lot * ways + distance,
                    peers[distance],
                )
                for distance in range(1, ways)
            ]

        def give_across(lot, copies):
            index, first, rows = chunks[lot]
            half = rows // 2
            for copy in copies:
                copy.wait_recv()
            mine = window(first + side * half, half, 0)
            return send(results[index].at[mine], results[index].at[mine], 5, lot, across)

        small_copy = small_round(0, small_copy)
        core_copy.wait_recv()
        pair_ref[...] = (own_ref[...] + core_in[...].astype(f32)).astype(bf16)
        chip_copy = send(pair_ref, chip_in, 6, 0, chip_to)
        mixed_copy = send(mixed_ref, mixed_out_ref.at[own_rows], 7, 0, core_to)
        mixed_own = pltpu.make_async_copy(mixed_ref, mixed_out_ref.at[own_rows], sems[-1].at[0])
        mixed_own.start()
        small_copy = small_round(1, small_copy)
        reduced, gathered, given = {}, {}, {}
        for step in range(lots + 4):
            if step + 3 < lots:
                start_across(step + 3)
            if step < lots:
                reduced[step] = reduce_across(step)
            if 2 <= step < lots + 2:
                gathered[step - 2] = reduce_places(step - 2, reduced[step - 2])
            if step >= 4:
                given[step - 4] = give_across(step - 4, gathered[step - 4])
            if step in (5, 9):
                small_copy = small_round(2 if step == 5 else 3, small_copy)
        chip_copy.wait_recv()
        strip = 64

        def norm_rows(at, none):
            first = pl.multiple_of(at * strip, strip)
            rows = pl.ds(first, strip)
            grad_norm = pair_ref[rows, :].astype(f32) + chip_in[rows, :].astype(f32)
            scaled = grad_norm * gain_ref[...]
            normed_rows = normed_ref[rows, :]
            grad_input = inverse_ref[rows, :] * (
                scaled
                - jnp.mean(scaled, axis=-1, keepdims=True)
                - normed_rows * jnp.mean(scaled * normed_rows, axis=-1, keepdims=True)
            )
            tokens_ref[pl.ds(pl.multiple_of(mine_first + first, strip), strip), :] = (
                resid_ref[rows, :] + grad_input
            ).astype(bf16)
            return none

        lax.fori_loop(0, own_ref.shape[0] // strip, norm_rows, 0)
        tokens_copy = send(tokens_ref.at[own_rows], tokens_ref.at[own_rows], 8, 0, core_to)
        small_round(4, small_copy)
        mixed_own.wait()
        mixed_copy.wait_recv()
        tokens_copy.wait_recv()
        for lot in range(lots):
            given[lot].wait_recv()
        for copy in pending:
            copy.wait_send()

    vmem = pl.BlockSpec(memory_space=pltpu.VMEM)
    shapes = [jax.ShapeDtypeStruct(grad.shape, bf16) for grad in grads]
    both = jax.ShapeDtypeStruct((2 * own_part.shape[0], own_part.shape[1]), bf16)
    shapes += [both, both, jax.ShapeDtypeStruct(small.shape, f32)]
    wide = [grads[index].shape[1] for index, _, _ in chunks]
    scratch = [pltpu.VMEM((lot[2] // 2, w), bf16) for lot, w in zip(chunks, wide)]
    scratch += [pltpu.VMEM((lot[2] // 2, w), bf16) for lot, w in zip(chunks, wide)]
    scratch += [pltpu.VMEM((ways - 1, lot[2] // 2 // ways, w), bf16) for lot, w in zip(chunks, wide)]
    scratch += [pltpu.VMEM(far_part.shape, bf16)] * 3
    scratch += [pltpu.VMEM((rounds,) + small.shape, f32)] * 2
    for number_of in (1, rounds, lots, lots * ways, lots * ways, lots, 1, 1, 1):
        scratch += [pltpu.SemaphoreType.DMA((number_of,))] * 2
    scratch.append(pltpu.SemaphoreType.DMA((1,)))
    return pl.pallas_call(
        kernel,
        in_specs=[vmem] * (len(grads) + 8),
        out_specs=[vmem] * len(shapes),
        out_shape=shapes,
        scratch_shapes=scratch,
        compiler_params=pltpu.CompilerParams(
            collective_id=number, has_side_effects=True, vmem_limit_bytes=44 << 20
        ),
        cost_estimate=pl.CostEstimate(flops=0, bytes_accessed=150 << 20, transcendentals=0),
    )(*grads, far_part, own_part, small, normed, inverse, gain, resid, mixed)


def shards(
    tokens,
    views,
    ln1_gain,
    ln1_bias,
    w_query,
    w_key,
    w_value,
    w_out,
    ln2_gain,
    ln2_bias,
    w_up,
    w_down,
    cotangent,
):
    row_count, width = tokens.shape
    inner = w_query.shape[1]
    heads = inner // HEAD_DIM
    half = row_count // 2
    group = MAX_VIEWS * VIEW_TOK // row_count
    devices = lax.axis_size("dp")
    assert row_count == VIEW_TOK and group == 2 * heads and lax.axis_size("tensor") == 4
    position = lax.axis_index("dp")
    block = position % group
    side = block % 2
    core = lax.axis_index("tensor") % 2
    scene_views = lax.dynamic_index_in_dim(views, position // group, keepdims=False)
    own_views = ((scene_views + 1 - side) // 2).reshape(1)
    far_views = ((scene_views + side) // 2).reshape(1)
    keep = (block < scene_views).astype(f32)
    def across(block):
        return lax.ppermute(block, "dp", [(i, i ^ 1) for i in range(devices)])

    def other_core(block):
        return lax.ppermute(block, "tensor", [(i, i ^ 1) for i in range(4)])

    def other_chip(block):
        return lax.ppermute(block, "tensor", [(i, i ^ 2) for i in range(4)])

    def own_first(block):
        return jnp.where(core == 0, block, jnp.concatenate([block[half:], block[:half]], axis=0))

    def pair_sum(far_part, own_part):
        arrived = other_core(far_part.astype(bf16))
        return (own_part + arrived.astype(f32)).astype(bf16)

    def both_halves(own):
        return jnp.concatenate([own, other_core(own)], axis=0)

    grad_rows = own_first(cotangent)
    inputs_own = jnp.where(core == 0, tokens[:half], tokens[half:]).astype(f32)
    grad_own = grad_rows[:half].astype(f32)

    attn_in, normed_first, inverse_first = first_norm(core, tokens, ln1_gain, ln1_bias)
    w_pairs = jnp.concatenate(
        [w_key.reshape(width, heads, HEAD_DIM), w_value.reshape(width, heads, HEAD_DIM)], axis=2
    ).reshape(width, 2 * inner)
    kv_low = dot(attn_in, w_pairs).astype(bf16)
    query_low = (contract(w_query, attn_in, 0, 1) * (LOG2E * HEAD_DIM ** (-0.5))).astype(bf16)
    q_cols, kv_own = exchange(1, heads, (query_low, 0, 1), (kv_low, 1, 0))
    kv_far = across(kv_own)

    carry = sweep_forward(own_views, q_cols, kv_own, None, False)
    heads_out, heads_low, log_norm = sweep_forward(far_views, q_cols, kv_far, carry, True)
    (attn_cols,) = exchange(2, heads, (heads_low, 1, 0))

    pair = pair_sum(
        contract(attn_cols[:, half:], w_out, 0, 0), contract(attn_cols[:, :half], w_out, 0, 0)
    )
    resid = inputs_own + keep * (pair.astype(f32) + other_chip(pair).astype(f32))
    mlp_norm, normed_second, inverse_second = layer_norm(resid, ln2_gain, ln2_bias)
    mlp_in = both_halves(mlp_norm.astype(bf16))
    grad_mlp = (keep * grad_rows.astype(f32)).astype(bf16)
    grad_act = lax.optimization_barrier(contract(grad_mlp, w_down, 1, 1))
    up_proj = dot(mlp_in, w_up)
    activated, gelu_pull = jax.vjp(partial(jax.nn.gelu, approximate=True), up_proj)
    act_low = activated.astype(bf16)
    grad_up = gelu_pull(grad_act)[0].astype(bf16)
    pair = pair_sum(contract(grad_up[half:], w_up, 1, 1), contract(grad_up[:half], w_up, 1, 1))
    w_down_grad = contract(act_low, grad_mlp, 0, 0).astype(bf16)
    w_up_grad = contract(mlp_in, grad_up, 0, 0).astype(bf16)
    arrived, act_low, w_up_grad, w_down_grad = lax.optimization_barrier(
        (other_chip(pair), act_low, w_up_grad, w_down_grad)
    )
    grad_mlp_in = pair.astype(f32) + arrived.astype(f32)
    mlp_pair = pair_sum(dot(act_low[half:], w_down), dot(act_low[:half], w_down))
    mlp_arrived = other_chip(mlp_pair)
    grad_second, ln2_gain_grad, ln2_bias_grad = norm_back(
        grad_mlp_in, normed_second, inverse_second, ln2_gain
    )
    grad_resid = grad_own + grad_second
    grad_attn = both_halves((keep * grad_resid).astype(bf16))
    grad_heads = contract(w_out, grad_attn, 1, 1).astype(bf16)
    (g_cols,) = exchange(3, heads, (grad_heads, 0, 1))
    w_out_grad = dot(attn_cols, grad_attn).astype(bf16)

    bias = None
    if devices > group:
        seen = 2 * jnp.arange(heads, dtype=jnp.int32)
        seen = jnp.concatenate([seen + 1 - side, seen + side])
        bias = jnp.where(seen < scene_views, 0.0, -1e30).astype(f32)
    pairs, dq_cols, w_up_grad, w_down_grad = sweep_backward(
        6,
        heads,
        bias,
        q_cols,
        g_cols,
        heads_out,
        kv_far,
        kv_own,
        log_norm,
        (w_up_grad, w_down_grad),
    )
    resid, mlp_pair, mlp_arrived, pairs = lax.optimization_barrier(
        (resid, mlp_pair, mlp_arrived, pairs)
    )
    mixed_own = (
        resid + keep * (mlp_pair.astype(f32) + mlp_arrived.astype(f32))
    ).astype(bf16)
    grad_query, grad_pairs = exchange(4, heads, (dq_cols, 1, 0), (pairs, 0, 1))

    def partial_in(start):
        return contract(grad_query[:, start : start + half], w_query, 0, 1) + contract(
            grad_pairs[start : start + half], w_pairs, 1, 1
        )

    far_part, own_part = partial_in(half), partial_in(0)
    small = jnp.stack(
        [
            jnp.sum(far_part * normed_first[half:], axis=0)
            + jnp.sum(own_part * normed_first[:half], axis=0),
            jnp.sum(far_part, axis=0) + jnp.sum(own_part, axis=0),
            ln2_gain_grad * 0.5,
            ln2_bias_grad * 0.5,
        ]
        + [jnp.zeros((width,), f32)] * 4
    )
    late = (
        w_out_grad,
        contract(attn_in, grad_pairs, 0, 0).astype(bf16),
        contract(attn_in, grad_query, 0, 1).astype(bf16),
    )
    w_out_grad, w_pairs_grad, w_query_grad, tokens_grad, mixed, small = last_sums(
        5,
        heads,
        late,
        far_part.astype(bf16),
        own_part,
        small,
        normed_first[:half],
        inverse_first[:half],
        ln1_gain.reshape(1, width),
        grad_resid,
        mixed_own,
    )
    if devices > group:
        same = [list(range(at, devices, group)) for at in range(group)]
        w_out_grad, w_pairs_grad, w_query_grad, w_up_grad, w_down_grad, small = [
            lax.psum(array, "dp", axis_index_groups=same)
            for array in (
                w_out_grad,
                w_pairs_grad,
                w_query_grad,
                w_up_grad,
                w_down_grad,
                small,
            )
        ]
    w_pairs_grad = w_pairs_grad.astype(f32).reshape(width, heads, 2 * HEAD_DIM)

    return (
        mixed,
        tokens_grad,
        small[0],
        small[1],
        w_query_grad.astype(f32),
        w_pairs_grad[:, :, :HEAD_DIM].reshape(width, inner),
        w_pairs_grad[:, :, HEAD_DIM:].reshape(width, inner),
        w_out_grad.astype(f32),
        small[2],
        small[3],
        w_up_grad.astype(f32),
        w_down_grad.astype(f32),
    )


def solution(mesh):
    placed = (
        P("dp", None),
        P(),
        P(),
        P(),
        P(None, "tensor"),
        P(None, "tensor"),
        P(None, "tensor"),
        P("tensor", None),
        P(),
        P(),
        P(None, "tensor"),
        P("tensor", None),
        P("dp", None),
    )
    return jax.shard_map(
        shards,
        mesh=mesh,
        in_specs=placed,
        out_specs=(
            P("dp", None),
            P("dp", None),
            P(),
            P(),
            P(None, "tensor"),
            P(None, "tensor"),
            P(None, "tensor"),
            P("tensor", None),
            P(),
            P(),
            P(None, "tensor"),
            P("tensor", None),
        ),
        check_vma=False,
    )
```

```python
from functools import partial
import math

import jax
import jax.numpy as jnp
from jax import lax
from jax.experimental import pallas as pl
from jax.experimental.pallas import tpu as pltpu
from jax.sharding import PartitionSpec as P

HEAD_DIM = 64
VIEW_TOK = 1024
MAX_VIEWS = 8
LOG2E = math.log2(math.e)
VMEM_BYTES = 48 << 20
LOT = 128 << 10

norm_eps = 1e-05

bf16 = jnp.bfloat16
f32 = jnp.float32
dot = partial(jnp.dot, preferred_element_type=f32)


def contract(left, right, left_dim, right_dim):
    return lax.dot_general(
        left, right, (((left_dim,), (right_dim,)), ((), ())), preferred_element_type=f32
    )


def layer_norm(values, gain, shift):
    row_mean = jnp.mean(values, axis=-1, keepdims=True)
    centered = values - row_mean
    inverse = lax.rsqrt(jnp.mean(centered * centered, axis=-1, keepdims=True) + norm_eps)
    normed = centered * inverse
    return (normed * gain + shift, normed, inverse)


def norm_back(grad_norm, normed, inverse, gain):
    scaled = grad_norm * gain
    grad_input = inverse * (
        scaled
        - jnp.mean(scaled, axis=-1, keepdims=True)
        - normed * jnp.mean(scaled * normed, axis=-1, keepdims=True)
    )
    return (grad_input, jnp.sum(grad_norm * normed, axis=0), jnp.sum(grad_norm, axis=0))


def first_norm(core, tokens, gain, shift):
    row_count, width = tokens.shape
    block = row_count // 4

    def kernel(core_ref, tokens_ref, gain_ref, shift_ref, out_ref, normed_ref, inverse_ref):
        values, normed, inverse = layer_norm(
            tokens_ref[...].astype(f32), gain_ref[...], shift_ref[...]
        )
        out_ref[...] = values.astype(bf16)
        normed_ref[...] = normed
        inverse_ref[...] = inverse

    by_rows = pl.BlockSpec((block, width), lambda i, core_ref: (i, 0))
    row = pl.BlockSpec((1, width), lambda i, core_ref: (0, 0))
    return pl.pallas_call(
        kernel,
        grid_spec=pltpu.PrefetchScalarGridSpec(
            num_scalar_prefetch=1,
            grid=(4,),
            in_specs=[
                pl.BlockSpec((block, width), lambda i, core_ref: ((i + 2 * core_ref[0]) % 4, 0)),
                row,
                row,
            ],
            out_specs=[by_rows, by_rows, pl.BlockSpec((block, 1), lambda i, core_ref: (i, 0))],
        ),
        out_shape=[
            jax.ShapeDtypeStruct((row_count, width), bf16),
            jax.ShapeDtypeStruct((row_count, width), f32),
            jax.ShapeDtypeStruct((row_count, 1), f32),
        ],
        cost_estimate=pl.CostEstimate(
            flops=10 * row_count * width, bytes_accessed=8 * row_count * width, transcendentals=0
        ),
    )(core.reshape(1).astype(jnp.int32), tokens, gain.reshape(1, width), shift.reshape(1, width))


def sweep_forward(live_views, q_cols, kv, carry, last):
    count = q_cols.shape[1]
    keys = kv.shape[0]
    sum_rows = HEAD_DIM + 16
    bq, bk = 2048, 512

    def kernel(*refs):
        live_ref, q_ref, kv_ref = refs[:3]
        columns_ref = refs[-1]
        refs = refs[3:-1]
        if carry is not None:
            start = (refs[0][...], refs[1][...])
            refs = refs[2:]
        else:
            start = (jnp.full((1, bq), -1e30, f32), jnp.zeros((sum_rows, bq), f32))
        queries = jnp.concatenate([q_ref[...], jnp.zeros((HEAD_DIM, bq), bf16)], axis=0)

        @pl.when(pl.program_id(0) == 0)
        def _():
            columns_ref[HEAD_DIM:, :] = jnp.ones((16, keys), bf16)
            columns_ref[:HEAD_DIM, :] = kv_ref[...].T[HEAD_DIM:]

        def view_step(view, running):
            top, accum = running
            for part in range(VIEW_TOK // bk):
                first = pl.multiple_of(view * VIEW_TOK + part * bk, bk)
                scores = dot(kv_ref[pl.ds(first, bk), :], queries)
                new_top = jnp.maximum(top, jnp.max(scores, axis=0, keepdims=True))
                weights = jnp.exp2(scores - new_top).astype(bf16)
                accum = accum * jnp.exp2(top - new_top) + dot(
                    columns_ref[:, pl.ds(first, bk)], weights
                )
                top = new_top
            return (top, accum)

        top, accum = lax.fori_loop(0, live_ref[0], view_step, start)
        if last:
            total = accum[HEAD_DIM : HEAD_DIM + 1]
            heads_out = accum[:HEAD_DIM] / total
            refs[0][...] = heads_out
            refs[1][...] = heads_out.astype(bf16)
            refs[2][...] = top + jnp.log2(total)
        else:
            refs[0][...] = top
            refs[1][...] = accum

    def columns(rows):
        return pl.BlockSpec((rows, bq), lambda i: (0, i))

    in_specs = [
        pl.BlockSpec(memory_space=pltpu.SMEM),
        columns(HEAD_DIM),
        pl.BlockSpec(kv.shape, lambda i: (0, 0)),
    ]
    operands = [live_views, q_cols, kv]
    if carry is not None:
        in_specs += [columns(1), columns(sum_rows)]
        operands += list(carry)
    if last:
        shapes = [((HEAD_DIM, count), f32), ((HEAD_DIM, count), bf16), ((1, count), f32)]
    else:
        shapes = [((1, count), f32), ((sum_rows, count), f32)]
    return pl.pallas_call(
        kernel,
        grid=(count // bq,),
        in_specs=in_specs,
        out_specs=[columns(shape[0]) for shape, _ in shapes],
        out_shape=[jax.ShapeDtypeStruct(shape, kind) for shape, kind in shapes],
        scratch_shapes=[pltpu.VMEM((sum_rows, keys), bf16)],
        compiler_params=pltpu.CompilerParams(vmem_limit_bytes=VMEM_BYTES),
        cost_estimate=pl.CostEstimate(
            flops=16 * HEAD_DIM * count * keys, bytes_accessed=8 << 20, transcendentals=count * keys
        ),
    )(*operands)


MESH = pl.DeviceIdType.MESH


def greet(peers):
    barrier = pltpu.get_barrier_semaphore()
    for peer in peers:
        pl.semaphore_signal(barrier, inc=1, device_id=peer, device_id_type=MESH)
    pl.semaphore_wait(barrier, len(peers))


def window(start, size, axis):
    span = pl.ds(pl.multiple_of(start, size), size)
    return (span, slice(None)) if axis == 0 else (slice(None), span)


def exchange(number, ways, *items):
    def kernel(*refs):
        count = len(items)
        sources, targets = refs[:count], refs[count : 2 * count]
        own_sems, send_sems, recv_sems = refs[2 * count :]
        position = lax.axis_index("dp")
        place = position % (2 * ways) // 2
        base = position - 2 * place
        places = [lax.rem(place + distance, ways) for distance in range(ways)]
        greet([{"dp": base + 2 * places[distance]} for distance in range(1, ways)])
        copies = []
        for distance in range(1, ways):
            for index, (array, split, concat) in enumerate(items):
                size = array.shape[split] // ways
                copy = pltpu.make_async_remote_copy(
                    src_ref=sources[index].at[window(places[distance] * size, size, split)],
                    dst_ref=targets[index].at[
                        window(place * array.shape[concat], array.shape[concat], concat)
                    ],
                    send_sem=send_sems.at[index, distance],
                    recv_sem=recv_sems.at[index, distance],
                    device_id={"dp": base + 2 * places[distance]},
                    device_id_type=MESH,
                )
                copy.start()
                copies.append(copy)
        for index, (array, split, concat) in enumerate(items):
            size = array.shape[split] // ways
            copy = pltpu.make_async_copy(
                sources[index].at[window(place * size, size, split)],
                targets[index].at[
                    window(place * array.shape[concat], array.shape[concat], concat)
                ],
                own_sems.at[index],
            )
            copy.start()
            copies.append(copy)
        for copy in copies:
            copy.wait()

    def shape(array, split, concat):
        sizes = list(array.shape)
        sizes[split] //= ways
        sizes[concat] *= ways
        return jax.ShapeDtypeStruct(tuple(sizes), array.dtype)

    count = len(items)
    vmem = pl.BlockSpec(memory_space=pltpu.VMEM)
    moved = sum(array.size * array.dtype.itemsize for array, _, _ in items)
    return pl.pallas_call(
        kernel,
        in_specs=[vmem] * count,
        out_specs=[vmem] * count,
        out_shape=[shape(*item) for item in items],
        scratch_shapes=[
            pltpu.SemaphoreType.DMA((count,)),
            pltpu.SemaphoreType.DMA((count, ways)),
            pltpu.SemaphoreType.DMA((count, ways)),
        ],
        compiler_params=pltpu.CompilerParams(
            collective_id=number, has_side_effects=True, vmem_limit_bytes=16 << 20
        ),
        cost_estimate=pl.CostEstimate(flops=0, bytes_accessed=40 * moved, transcendentals=0),
    )(*[array for array, _, _ in items])


def sweep_backward(number, ways, bias, q_cols, g_cols, heads_out, kv_far, kv_own, log_norm, grads):
    count = q_cols.shape[1]
    keys = kv_own.shape[0]
    bq, bk = 1024, 512
    steps = 2 * keys // VIEW_TOK
    rows_of, width = grads[0].shape
    lot_rows = rows_of // steps
    half, part = lot_rows // 2, lot_rows // 2 // ways

    def kernel(*refs):
        masked = bias is not None
        bias_ref = refs[0] if masked else None
        refs = refs[1:] if masked else refs
        q_ref, g_ref, heads_ref, far_ref, own_ref, norm_ref = refs[:6]
        sources, home_ref, query_ref, results = refs[6:8], refs[8], refs[9], refs[10:12]
        total_ref, rows_ref, delta_ref, kv_ref, given_ref, met_ref, x_in, x_sums, z_in = refs[12:21]
        pairs_ref, low_ref = refs[21:23]
        sems = refs[23:]
        position = lax.axis_index("dp")
        place = position % (2 * ways) // 2
        side = position % 2
        base = position - 2 * place
        across = {"dp": position + 1 - 2 * side}
        places = [lax.rem(place + distance, ways) for distance in range(ways)]
        peers = [{"dp": base + 2 * at} for at in places]
        greet([across] + peers[1:])

        def remote(source, target, kind, at, to):
            return pltpu.make_async_remote_copy(
                src_ref=source,
                dst_ref=target,
                send_sem=sems[2 * kind].at[at],
                recv_sem=sems[2 * kind + 1].at[at],
                device_id=to,
                device_id_type=MESH,
            )

        def over_x(which, lot):
            given = window(lot * lot_rows + (1 - side) * half, half, 0)
            slot = which * steps + lot
            return remote(sources[which].at[given], x_in.at[slot], 0, slot, across)

        def to_places(which, lot, distance):
            slot = which * steps + lot
            return remote(
                x_sums.at[slot, window(places[distance] * part, part, 0)[0]],
                z_in.at[slot, distance - 1],
                1,
                slot * ways + distance,
                peers[distance],
            )

        def from_place(which, lot, distance):
            slot = which * steps + lot
            mine = results[which].at[window(lot * lot_rows + side * half + place * part, part, 0)]
            return remote(mine, mine, 2, slot * ways + distance, peers[distance])

        def back_over_x(which, lot):
            mine = results[which].at[window(lot * lot_rows + side * half, half, 0)]
            return remote(mine, mine, 3, which * steps + lot, across)

        def far_pairs(view):
            span = window(view * VIEW_TOK, VIEW_TOK, 0)
            return remote(given_ref.at[span], met_ref.at[span], 4, view, across)

        def pairs_home(distance):
            span = window(lax.rem(place + distance, ways) * VIEW_TOK, VIEW_TOK, 0)
            return (
                pairs_ref.at[span],
                home_ref.at[window(place * 2 * HEAD_DIM, 2 * HEAD_DIM, 1)],
                5,
                distance,
                {"dp": base + 2 * lax.rem(place + distance, ways)},
            )

        def query_home(distance):
            span = window(places[distance] * VIEW_TOK, VIEW_TOK, 1)
            return (
                low_ref.at[span],
                query_ref.at[window(place * HEAD_DIM, HEAD_DIM, 0)],
                6,
                distance,
                peers[distance],
            )

        def start_lot(lot):
            for which in range(2):
                over_x(which, lot).start()

        def reduce_across(lot):
            for which in range(2):
                slot = which * steps + lot
                over_x(which, lot).wait_recv()
                kept = sources[which][window(lot * lot_rows + side * half, half, 0)]
                x_sums[slot] = (kept.astype(f32) + x_in[slot].astype(f32)).astype(bf16)
                for distance in range(1, ways):
                    to_places(which, lot, distance).start()

        def reduce_places(lot):
            for which in range(2):
                slot = which * steps + lot
                total = x_sums[slot, window(place * part, part, 0)[0], :].astype(f32)
                for distance in range(1, ways):
                    to_places(which, lot, distance).wait_recv()
                    total += z_in[slot, distance - 1].astype(f32)
                mine = window(lot * lot_rows + side * half + place * part, part, 0)
                results[which][mine] = total.astype(bf16)
                for distance in range(1, ways):
                    from_place(which, lot, distance).start()

        def give_across(lot):
            for which in range(2):
                for distance in range(1, ways):
                    from_place(which, lot, distance).wait_recv()
                back_over_x(which, lot).start()

        start_lot(0)
        start_lot(1)
        total_ref[...] = jnp.zeros_like(total_ref)
        rows_ref[...] = jnp.concatenate([q_ref[...], g_ref[...]], axis=0).T
        delta_ref[...] = jnp.sum(g_ref[...].astype(f32) * heads_ref[...], axis=0, keepdims=True)
        kv_ref[:keys, :] = far_ref[...]
        kv_ref[keys:, :] = own_ref[...]

        def view_of(step):
            return lax.rem(place + 1 + lax.rem(step, ways), ways)

        def key_block(step, at):
            view = view_of(step)
            own = step // ways
            first = pl.multiple_of(view * VIEW_TOK + at * bk, bk)
            rows_here = pl.ds(first, bk)
            key_values = kv_ref[pl.ds(pl.multiple_of(own * keys + first, bk), bk), :]
            key_columns = key_values.T[:HEAD_DIM]
            empty = jnp.zeros((HEAD_DIM, bq), bf16)
            is_key = lax.broadcasted_iota(jnp.int32, (bq, 2 * HEAD_DIM), 1) < HEAD_DIM

            def parts(pair, accum):
                for bit in range(2):
                    span = pl.ds(pl.multiple_of((pair * 2 + bit) * bq, bq), bq)
                    scores = dot(key_values, jnp.concatenate([q_ref[:, span], empty], axis=0))
                    if masked:
                        scores += bias_ref[own * ways + view]
                    weights = jnp.exp2(scores - norm_ref[:, span])
                    grad_weights = dot(
                        key_values, jnp.concatenate([empty, g_ref[:, span]], axis=0)
                    )
                    grad_scores = (weights * (grad_weights - delta_ref[:, span])).astype(bf16)
                    rows = rows_ref[span, :]
                    none = jnp.zeros_like(rows)
                    accum += dot(weights.astype(bf16), jnp.where(is_key, none, rows))
                    accum += dot(grad_scores, jnp.where(is_key, rows, none))
                    total_ref[:, span] += dot(key_columns, grad_scores)
                return accum

            accum = lax.fori_loop(
                0, count // (2 * bq), parts, jnp.zeros((bk, 2 * HEAD_DIM), f32)
            )
            lane = lax.broadcasted_iota(jnp.int32, accum.shape, 1)
            accum = jnp.where(lane < HEAD_DIM, accum * (1.0 / LOG2E), accum)

            @pl.when(step < steps // 2)
            def _():
                given_ref[rows_here, :] = accum.astype(bf16)

            @pl.when(step >= steps // 2)
            def _():
                pairs_ref[rows_here, :] = (accum + met_ref[rows_here, :].astype(f32)).astype(bf16)

        def view_step(step, none):
            @pl.when(step + 2 < steps)
            def _():
                start_lot(step + 2)

            reduce_across(step)

            @pl.when(step >= 1)
            def _():
                reduce_places(step - 1)

            @pl.when(step >= 2)
            def _():
                give_across(step - 2)

            @pl.when(step >= steps // 2)
            def _():
                far_pairs(view_of(step)).wait_recv()

            def blocks(at, none):
                key_block(step, at)
                return none

            lax.fori_loop(0, VIEW_TOK // bk, blocks, 0)

            @pl.when(step < steps // 2)
            def _():
                far_pairs(view_of(step)).start()

            @pl.when(jnp.logical_and(step >= steps // 2, step < steps - 1))
            def _():
                remote(*pairs_home(step + 1 - steps // 2)).start()

            return none

        lax.fori_loop(0, steps, view_step, 0)
        reduce_places(steps - 1)
        low_ref[...] = (total_ref[...] * HEAD_DIM ** (-0.5)).astype(bf16)
        for distance in range(1, ways):
            remote(*query_home(distance)).start()
        mine = pltpu.make_async_copy(*pairs_home(0)[:2], sems[-1].at[0])
        mine.start()
        mine_too = pltpu.make_async_copy(*query_home(0)[:2], sems[-1].at[1])
        mine_too.start()
        give_across(steps - 2)
        give_across(steps - 1)
        mine.wait()
        mine_too.wait()
        for distance in range(1, ways):
            remote(*pairs_home(distance)).wait()
            remote(*query_home(distance)).wait()

        def finish(lot, none):
            for which in range(2):
                over_x(which, lot).wait_send()
                back_over_x(which, lot).wait_recv()
                back_over_x(which, lot).wait_send()
                for distance in range(1, ways):
                    to_places(which, lot, distance).wait_send()
                    from_place(which, lot, distance).wait_send()

            return none

        lax.fori_loop(0, steps, finish, 0)
        for view in range(steps // 2):
            far_pairs(view).wait_send()

    vmem = pl.BlockSpec(memory_space=pltpu.VMEM)
    operands = [q_cols, g_cols, heads_out, kv_far, kv_own, log_norm] + list(grads)
    in_specs = [vmem] * len(operands)
    if bias is not None:
        operands = [bias] + operands
        in_specs = [pl.BlockSpec(memory_space=pltpu.SMEM)] + in_specs
    lots = 2 * steps
    scratch = [
        pltpu.VMEM((HEAD_DIM, count), f32),
        pltpu.VMEM((count, 2 * HEAD_DIM), bf16),
        pltpu.VMEM((1, count), f32),
        pltpu.VMEM((2 * keys, 2 * HEAD_DIM), bf16),
        pltpu.VMEM((keys, 2 * HEAD_DIM), bf16),
        pltpu.VMEM((keys, 2 * HEAD_DIM), bf16),
        pltpu.VMEM((lots, half, width), bf16),
        pltpu.VMEM((lots, half, width), bf16),
        pltpu.VMEM((lots, ways - 1, part, width), bf16),
        pltpu.VMEM((keys, 2 * HEAD_DIM), bf16),
        pltpu.VMEM((HEAD_DIM, count), bf16),
    ]
    for number_of in (lots, lots * ways, lots * ways, lots, steps // 2, ways, ways):
        scratch += [pltpu.SemaphoreType.DMA((number_of,))] * 2
    scratch.append(pltpu.SemaphoreType.DMA((2,)))
    return pl.pallas_call(
        kernel,
        in_specs=in_specs,
        out_specs=[vmem] * 4,
        out_shape=[
            jax.ShapeDtypeStruct((VIEW_TOK, ways * 2 * HEAD_DIM), bf16),
            jax.ShapeDtypeStruct((ways * HEAD_DIM, VIEW_TOK), bf16),
        ]
        + [jax.ShapeDtypeStruct(grad.shape, bf16) for grad in grads],
        scratch_shapes=scratch,
        compiler_params=pltpu.CompilerParams(
            collective_id=number, has_side_effects=True, vmem_limit_bytes=VMEM_BYTES
        ),
        cost_estimate=pl.CostEstimate(
            flops=80 * HEAD_DIM * count * keys,
            bytes_accessed=20 << 20,
            transcendentals=2 * count * keys,
        ),
    )(*operands)


def last_sums(number, ways, grads, far_part, own_part, small, normed, inverse, gain, resid, mixed):
    chunks = []
    for index, grad in enumerate(grads):
        rows = grad.shape[0] * LOT // grad.size
        chunks += [(index, first, rows) for first in range(0, grad.shape[0], rows)]
    lots = len(chunks)
    rounds = 5

    def kernel(*refs):
        count = len(grads)
        sources = refs[:count]
        far_ref, own_ref, small_ref, normed_ref, inverse_ref, gain_ref, resid_ref, mixed_ref = refs[
            count : count + 8
        ]
        refs = refs[count + 8 :]
        results = refs[:count]
        tokens_ref, mixed_out_ref, small_sum_ref = refs[count : count + 3]
        refs = refs[count + 3 :]
        x_in, x_sums, z_in = refs[:lots], refs[lots : 2 * lots], refs[2 * lots : 3 * lots]
        core_in, pair_ref, chip_in, small_in, small_out = refs[3 * lots : 3 * lots + 5]
        sems = refs[3 * lots + 5 :]
        position = lax.axis_index("dp")
        slot = lax.axis_index("tensor")
        place = position % (2 * ways) // 2
        side = position % 2
        base = position - 2 * place
        across = {"dp": position + 1 - 2 * side}
        places = [lax.rem(place + distance, ways) for distance in range(ways)]
        peers = [{"dp": base + 2 * at} for at in places]
        partner = slot + 1 - 2 * lax.rem(slot, 2)
        chip = lax.rem(slot + 2, 4)
        core_to, chip_to = {"tensor": partner}, {"tensor": chip}
        even = place + 1 - 2 * lax.rem(place, 2)
        steps = [
            core_to,
            chip_to,
            across,
            {"dp": base + 2 * even},
            {"dp": base + 2 * lax.rem(place + 2, ways)},
        ]
        greet([across, core_to, chip_to] + peers[1:])
        pending = []

        def send(source, target, pair, at, to):
            copy = pltpu.make_async_remote_copy(
                src_ref=source,
                dst_ref=target,
                send_sem=sems[2 * pair].at[at],
                recv_sem=sems[2 * pair + 1].at[at],
                device_id=to,
                device_id_type=MESH,
            )
            copy.start()
            pending.append(copy)
            return copy

        mine_first = lax.rem(slot, 2) * own_ref.shape[0]
        own_rows = window(mine_first, own_ref.shape[0], 0)
        small_copy = send(small_ref, small_in.at[0], 1, 0, steps[0])
        core_copy = send(far_ref, core_in, 0, 0, core_to)
        across_copies = []

        def start_across(lot):
            index, first, rows = chunks[lot]
            half = rows // 2
            given = window(first + (1 - side) * half, half, 0)
            across_copies.append(send(sources[index].at[given], x_in[lot], 2, lot, across))

        for lot in range(3):
            start_across(lot)

        def small_round(at, copy):
            copy.wait_recv()
            total = (small_ref if at == 0 else small_out.at[at - 1])[...] + small_in[at]
            if at == rounds - 1:
                small_sum_ref[...] = total
                return None
            small_out[at] = total
            return send(small_out.at[at], small_in.at[at + 1], 1, at + 1, steps[at + 1])

        def reduce_across(lot):
            index, first, rows = chunks[lot]
            half, part = rows // 2, rows // 2 // ways
            across_copies[lot].wait_recv()
            kept = sources[index][window(first + side * half, half, 0)]
            x_sums[lot][...] = (kept.astype(f32) + x_in[lot][...].astype(f32)).astype(bf16)
            return [
                send(
                    x_sums[lot].at[window(places[distance] * part, part, 0)],
                    z_in[lot].at[distance - 1],
                    3,
                    lot * ways + distance,
                    peers[distance],
                )
                for distance in range(1, ways)
            ]

        def reduce_places(lot, copies):
            index, first, rows = chunks[lot]
            half, part = rows // 2, rows // 2 // ways
            total = x_sums[lot][window(place * part, part, 0)].astype(f32)
            for distance in range(1, ways):
                copies[distance - 1].wait_recv()
                total += z_in[lot][distance - 1].astype(f32)
            mine = window(first + side * half + place * part, part, 0)
            results[index][mine] = total.astype(bf16)
            return [
                send(
                    results[index].at[mine],
                    results[index].at[mine],
                    4,
                    lot * ways + distance,
                    peers[distance],
                )
                for distance in range(1, ways)
            ]

        def give_across(lot, copies):
            index, first, rows = chunks[lot]
            half = rows // 2
            for copy in copies:
                copy.wait_recv()
            mine = window(first + side * half, half, 0)
            return send(results[index].at[mine], results[index].at[mine], 5, lot, across)

        small_copy = small_round(0, small_copy)
        core_copy.wait_recv()
        pair_ref[...] = (own_ref[...] + core_in[...].astype(f32)).astype(bf16)
        chip_copy = send(pair_ref, chip_in, 6, 0, chip_to)
        mixed_copy = send(mixed_ref, mixed_out_ref.at[own_rows], 7, 0, core_to)
        mixed_own = pltpu.make_async_copy(mixed_ref, mixed_out_ref.at[own_rows], sems[-1].at[0])
        mixed_own.start()
        small_copy = small_round(1, small_copy)
        reduced, gathered, given = {}, {}, {}
        for step in range(lots + 4):
            if step + 3 < lots:
                start_across(step + 3)
            if step < lots:
                reduced[step] = reduce_across(step)
            if 2 <= step < lots + 2:
                gathered[step - 2] = reduce_places(step - 2, reduced[step - 2])
            if step >= 4:
                given[step - 4] = give_across(step - 4, gathered[step - 4])
            if step in (5, 9):
                small_copy = small_round(2 if step == 5 else 3, small_copy)
        chip_copy.wait_recv()
        strip = 64

        def norm_rows(at, none):
            first = pl.multiple_of(at * strip, strip)
            rows = pl.ds(first, strip)
            grad_norm = pair_ref[rows, :].astype(f32) + chip_in[rows, :].astype(f32)
            scaled = grad_norm * gain_ref[...]
            normed_rows = normed_ref[rows, :]
            grad_input = inverse_ref[rows, :] * (
                scaled
                - jnp.mean(scaled, axis=-1, keepdims=True)
                - normed_rows * jnp.mean(scaled * normed_rows, axis=-1, keepdims=True)
            )
            tokens_ref[pl.ds(pl.multiple_of(mine_first + first, strip), strip), :] = (
                resid_ref[rows, :] + grad_input
            ).astype(bf16)
            return none

        lax.fori_loop(0, own_ref.shape[0] // strip, norm_rows, 0)
        tokens_copy = send(tokens_ref.at[own_rows], tokens_ref.at[own_rows], 8, 0, core_to)
        small_round(4, small_copy)
        mixed_own.wait()
        mixed_copy.wait_recv()
        tokens_copy.wait_recv()
        for lot in range(lots):
            given[lot].wait_recv()
        for copy in pending:
            copy.wait_send()

    vmem = pl.BlockSpec(memory_space=pltpu.VMEM)
    shapes = [jax.ShapeDtypeStruct(grad.shape, bf16) for grad in grads]
    both = jax.ShapeDtypeStruct((2 * own_part.shape[0], own_part.shape[1]), bf16)
    shapes += [both, both, jax.ShapeDtypeStruct(small.shape, f32)]
    wide = [grads[index].shape[1] for index, _, _ in chunks]
    scratch = [pltpu.VMEM((lot[2] // 2, w), bf16) for lot, w in zip(chunks, wide)]
    scratch += [pltpu.VMEM((lot[2] // 2, w), bf16) for lot, w in zip(chunks, wide)]
    scratch += [pltpu.VMEM((ways - 1, lot[2] // 2 // ways, w), bf16) for lot, w in zip(chunks, wide)]
    scratch += [pltpu.VMEM(far_part.shape, bf16)] * 3
    scratch += [pltpu.VMEM((rounds,) + small.shape, f32)] * 2
    for number_of in (1, rounds, lots, lots * ways, lots * ways, lots, 1, 1, 1):
        scratch += [pltpu.SemaphoreType.DMA((number_of,))] * 2
    scratch.append(pltpu.SemaphoreType.DMA((1,)))
    return pl.pallas_call(
        kernel,
        in_specs=[vmem] * (len(grads) + 8),
        out_specs=[vmem] * len(shapes),
        out_shape=shapes,
        scratch_shapes=scratch,
        compiler_params=pltpu.CompilerParams(
            collective_id=number, has_side_effects=True, vmem_limit_bytes=44 << 20
        ),
        cost_estimate=pl.CostEstimate(flops=0, bytes_accessed=150 << 20, transcendentals=0),
    )(*grads, far_part, own_part, small, normed, inverse, gain, resid, mixed)


def shards(
    tokens,
    views,
    ln1_gain,
    ln1_bias,
    w_query,
    w_key,
    w_value,
    w_out,
    ln2_gain,
    ln2_bias,
    w_up,
    w_down,
    cotangent,
):
    row_count, width = tokens.shape
    inner = w_query.shape[1]
    heads = inner // HEAD_DIM
    half = row_count // 2
    group = MAX_VIEWS * VIEW_TOK // row_count
    devices = lax.axis_size("dp")
    assert row_count == VIEW_TOK and group == 2 * heads and lax.axis_size("tensor") == 4
    position = lax.axis_index("dp")
    block = position % group
    side = block % 2
    core = lax.axis_index("tensor") % 2
    scene_views = lax.dynamic_index_in_dim(views, position // group, keepdims=False)
    own_views = ((scene_views + 1 - side) // 2).reshape(1)
    far_views = ((scene_views + side) // 2).reshape(1)
    keep = (block < scene_views).astype(f32)
    def across(block):
        return lax.ppermute(block, "dp", [(i, i ^ 1) for i in range(devices)])

    def other_core(block):
        return lax.ppermute(block, "tensor", [(i, i ^ 1) for i in range(4)])

    def other_chip(block):
        return lax.ppermute(block, "tensor", [(i, i ^ 2) for i in range(4)])

    def own_first(block):
        return jnp.where(core == 0, block, jnp.concatenate([block[half:], block[:half]], axis=0))

    def pair_sum(far_part, own_part):
        arrived = other_core(far_part.astype(bf16))
        return (own_part + arrived.astype(f32)).astype(bf16)

    def both_halves(own):
        return jnp.concatenate([own, other_core(own)], axis=0)

    grad_rows = own_first(cotangent)
    inputs_own = jnp.where(core == 0, tokens[:half], tokens[half:]).astype(f32)
    grad_own = grad_rows[:half].astype(f32)

    attn_in, normed_first, inverse_first = first_norm(core, tokens, ln1_gain, ln1_bias)
    w_pairs = jnp.concatenate(
        [w_key.reshape(width, heads, HEAD_DIM), w_value.reshape(width, heads, HEAD_DIM)], axis=2
    ).reshape(width, 2 * inner)
    kv_low = dot(attn_in, w_pairs).astype(bf16)
    query_low = (contract(w_query, attn_in, 0, 1) * (LOG2E * HEAD_DIM ** (-0.5))).astype(bf16)
    q_cols, kv_own = exchange(1, heads, (query_low, 0, 1), (kv_low, 1, 0))
    kv_far = across(kv_own)

    carry = sweep_forward(own_views, q_cols, kv_own, None, False)
    heads_out, heads_low, log_norm = sweep_forward(far_views, q_cols, kv_far, carry, True)
    (attn_cols,) = exchange(2, heads, (heads_low, 1, 0))

    pair = pair_sum(
        contract(attn_cols[:, half:], w_out, 0, 0), contract(attn_cols[:, :half], w_out, 0, 0)
    )
    resid = inputs_own + keep * (pair.astype(f32) + other_chip(pair).astype(f32))
    mlp_norm, normed_second, inverse_second = layer_norm(resid, ln2_gain, ln2_bias)
    mlp_in = both_halves(mlp_norm.astype(bf16))
    grad_mlp = (keep * grad_rows.astype(f32)).astype(bf16)
    grad_act = lax.optimization_barrier(contract(grad_mlp, w_down, 1, 1))
    up_proj = dot(mlp_in, w_up)
    activated, gelu_pull = jax.vjp(partial(jax.nn.gelu, approximate=True), up_proj)
    act_low = activated.astype(bf16)
    grad_up = gelu_pull(grad_act)[0].astype(bf16)
    pair = pair_sum(contract(grad_up[half:], w_up, 1, 1), contract(grad_up[:half], w_up, 1, 1))
    w_down_grad = contract(act_low, grad_mlp, 0, 0).astype(bf16)
    w_up_grad = contract(mlp_in, grad_up, 0, 0).astype(bf16)
    arrived, act_low, w_up_grad, w_down_grad = lax.optimization_barrier(
        (other_chip(pair), act_low, w_up_grad, w_down_grad)
    )
    grad_mlp_in = pair.astype(f32) + arrived.astype(f32)
    mlp_pair = pair_sum(dot(act_low[half:], w_down), dot(act_low[:half], w_down))
    mlp_arrived = other_chip(mlp_pair)
    grad_second, ln2_gain_grad, ln2_bias_grad = norm_back(
        grad_mlp_in, normed_second, inverse_second, ln2_gain
    )
    grad_resid = grad_own + grad_second
    grad_attn = both_halves((keep * grad_resid).astype(bf16))
    grad_heads = contract(w_out, grad_attn, 1, 1).astype(bf16)
    (g_cols,) = exchange(3, heads, (grad_heads, 0, 1))
    w_out_grad = dot(attn_cols, grad_attn).astype(bf16)

    bias = None
    if devices > group:
        seen = 2 * jnp.arange(heads, dtype=jnp.int32)
        seen = jnp.concatenate([seen + 1 - side, seen + side])
        bias = jnp.where(seen < scene_views, 0.0, -1e30).astype(f32)
    grad_pairs, grad_query, w_up_grad, w_down_grad = sweep_backward(
        6,
        heads,
        bias,
        q_cols,
        g_cols,
        heads_out,
        kv_far,
        kv_own,
        log_norm,
        (w_up_grad, w_down_grad),
    )
    resid, mlp_pair, mlp_arrived, grad_query = lax.optimization_barrier(
        (resid, mlp_pair, mlp_arrived, grad_query)
    )
    mixed_own = (
        resid + keep * (mlp_pair.astype(f32) + mlp_arrived.astype(f32))
    ).astype(bf16)
    def partial_in(start):
        return contract(grad_query[:, start : start + half], w_query, 0, 1) + contract(
            grad_pairs[start : start + half], w_pairs, 1, 1
        )

    far_part, own_part = partial_in(half), partial_in(0)
    small = jnp.stack(
        [
            jnp.sum(far_part * normed_first[half:], axis=0)
            + jnp.sum(own_part * normed_first[:half], axis=0),
            jnp.sum(far_part, axis=0) + jnp.sum(own_part, axis=0),
            ln2_gain_grad * 0.5,
            ln2_bias_grad * 0.5,
        ]
        + [jnp.zeros((width,), f32)] * 4
    )
    late = (
        w_out_grad,
        contract(attn_in, grad_pairs, 0, 0).astype(bf16),
        contract(attn_in, grad_query, 0, 1).astype(bf16),
    )
    w_out_grad, w_pairs_grad, w_query_grad, tokens_grad, mixed, small = last_sums(
        5,
        heads,
        late,
        far_part.astype(bf16),
        own_part,
        small,
        normed_first[:half],
        inverse_first[:half],
        ln1_gain.reshape(1, width),
        grad_resid,
        mixed_own,
    )
    if devices > group:
        same = [list(range(at, devices, group)) for at in range(group)]
        w_out_grad, w_pairs_grad, w_query_grad, w_up_grad, w_down_grad, small = [
            lax.psum(array, "dp", axis_index_groups=same)
            for array in (
                w_out_grad,
                w_pairs_grad,
                w_query_grad,
                w_up_grad,
                w_down_grad,
                small,
            )
        ]
    w_pairs_grad = w_pairs_grad.astype(f32).reshape(width, heads, 2 * HEAD_DIM)

    return (
        mixed,
        tokens_grad,
        small[0],
        small[1],
        w_query_grad.astype(f32),
        w_pairs_grad[:, :, :HEAD_DIM].reshape(width, inner),
        w_pairs_grad[:, :, HEAD_DIM:].reshape(width, inner),
        w_out_grad.astype(f32),
        small[2],
        small[3],
        w_up_grad.astype(f32),
        w_down_grad.astype(f32),
    )


def solution(mesh):
    placed = (
        P("dp", None),
        P(),
        P(),
        P(),
        P(None, "tensor"),
        P(None, "tensor"),
        P(None, "tensor"),
        P("tensor", None),
        P(),
        P(),
        P(None, "tensor"),
        P("tensor", None),
        P("dp", None),
    )
    return jax.shard_map(
        shards,
        mesh=mesh,
        in_specs=placed,
        out_specs=(
            P("dp", None),
            P("dp", None),
            P(),
            P(),
            P(None, "tensor"),
            P(None, "tensor"),
            P(None, "tensor"),
            P("tensor", None),
            P(),
            P(),
            P(None, "tensor"),
            P("tensor", None),
        ),
        check_vma=False,
    )
```
